256 devices in a mesh: gx: 8 (over z), gy: 32 (over x, y, core).
Axes of the slice: x: 4, y: 4, z: 8, core: 2. Of those that a mesh axis runs over, the one named last changes fastest.
Arguments:
- offsets: float32 [2, 16, 512, 128], P(None, 'gx', 'gy'), may hold values from 0 to 1
- density: float32 [16, 512, 128], P('gx', 'gy'), may hold values from 0.99 to 1.01
- velocity: float32 [2, 16, 512, 128], P(None, 'gx', 'gy'), may hold values from -4 to 4
- counts: int32 [16, 512], P('gx', 'gy'), may hold values from 1 to 128
- walls: int32 [16, 512], P('gx', 'gy'), may hold values 0 or 1
Outputs:
- new_offsets: float32 [2, 16, 512, 128], P(None, 'gx', 'gy')
- new_density: float32 [16, 512, 128], P('gx', 'gy')
- new_velocity: float32 [2, 16, 512, 128], P(None, 'gx', 'gy')
The draws below stay inside these ranges and needn't reach their ends.
All inputs are finite; a program needn't handle non-finite values. No bound on the sum of `walls` on one device may be relied on, other than what follows from the above.
Results may differ from the reference program's by a relative error of at most 0.0001.
Values sent between devices are 32-bit elements; how exact they have to be, the bound alone decides.
A program may use at most 64 MiB of HBM per device.

```python
import math
import jax
import jax.numpy as jnp
from jax import lax

SLOTS = 128
ITERS = 3
NX = 16
NY = 512


def place_ends(values, stream_key, least, high):
    shape = values.shape
    spot = [jax.random.randint(jax.random.fold_in(stream_key, axis), (), 0, shape[axis]) for axis in range(len(shape))]
    values = values.at[tuple(spot)].set(least)
    longest = shape.index(max(shape))
    spot[longest] = (spot[longest] + 1) % shape[longest]
    return values.at[tuple(spot)].set(high)


def shard_levels(own_key, shape, cuts, least, top_value):
    gain = 1.0
    for axis_at, blocks in cuts:
        heights = jax.random.uniform(jax.random.fold_in(jax.random.fold_in(own_key, 6), axis_at), (blocks,), jnp.float32, least / len(cuts), top_value / len(cuts))
        gain = gain * jnp.repeat(jnp.exp(heights), shape[axis_at] // blocks).reshape((-1,) + (1,) * (len(shape) - 1 - axis_at))
    return gain


def centred(own_key, dims, scale, reach, cuts=(), kind=jnp.bfloat16):
    entries = jax.random.normal(own_key, dims, jnp.float32) * scale
    if len(cuts) > 0:
        entries = shard_levels(own_key, dims, cuts, -0.22, 0.18) * entries
    return jnp.clip(entries, min=-reach, max=reach).astype(kind)


def setup_inputs(seed: int = 0) -> dict:
    key_list = jax.random.split(jax.random.key(seed), 6)
    offsets = jnp.clip(1.0 * jax.random.uniform(key_list[0], (2, NX, NY, SLOTS), jnp.float32) ** shard_levels(key_list[0], (2, NX, NY, SLOTS), ((1, 8), (2, 32)), -0.2, 0.2), 0.0, 1.0)
    density = jnp.clip(0.99 + 0.01999998 * jax.random.uniform(key_list[1], (NX, NY, SLOTS), jnp.float32) ** shard_levels(key_list[1], (NX, NY, SLOTS), ((0, 8), (1, 32)), -0.2, 0.2), 0.99, 1.01)
    velocity = centred(key_list[2], (2, NX, NY, SLOTS), 1.0, 4.0, ((1, 8), (2, 32)), jnp.float32)
    counts = place_ends(jax.random.randint(key_list[3], (NX, NY), 1, SLOTS + 1), jax.random.fold_in(key_list[3], 1), 1, SLOTS).astype(jnp.int32)
    walls = place_ends((jax.random.randint(key_list[4], (NX, NY), 0, 8) < 1).astype(jnp.int32), jax.random.fold_in(key_list[4], 1), 0, 1)
    return {"offsets": offsets, "density": density, "velocity": velocity, "counts": counts, "walls": walls}


sound_speed = 10.0
stiffness = 100.0
courant = 0.2
smoothing = 0.1625
volume = 1.0 / 64.0
kernel_norm = 7.0 / (4.0 * math.pi * smoothing * smoothing)
grad_coef = -5.0 * kernel_norm / (smoothing * smoothing)
regular_sq = 0.01 * smoothing * smoothing
gravity_accel = 9.81

def pair_rates(fields, occ_pad):
    rows = fields.shape[1] - 2
    width = fields.shape[2] - 2

    def one_row(row_index):
        block = lax.dynamic_slice_in_dim(fields, row_index, 3, 1)
        occ_block = lax.dynamic_slice_in_dim(occ_pad, row_index, 3, 0)
        own = block[:, 1, 1:width + 1]
        own_occ = occ_block[1, 1:width + 1]
        own_rho = own[2] + 1.0 - own_occ
        total_rho = jnp.zeros(own[0].shape, jnp.float32)
        total_x = jnp.zeros(own[0].shape, jnp.float32)
        total_y = jnp.zeros(own[0].shape, jnp.float32)
        for shift_x in (-1, 0, 1):
            for shift_y in (-1, 0, 1):
                other = block[:, 1 + shift_x, 1 + shift_y:1 + shift_y + width]
                other_occ = occ_block[1 + shift_x, 1 + shift_y:1 + shift_y + width]
                weight = volume * other_occ / (other[2] + 1.0 - other_occ)
                delta_x = own[0][:, :, None] - other[0][:, None, :] - float(shift_x)
                delta_y = own[1][:, :, None] - other[1][:, None, :] - float(shift_y)
                dist_sq = delta_x * delta_x + delta_y * delta_y
                dist = jnp.sqrt(dist_sq)
                support = jnp.maximum(1.0 - 0.5 * dist / smoothing, 0.0)
                grad_mag = grad_coef * support * support * support
                rel_x = own[3][:, :, None] - other[3][:, None, :]
                rel_y = own[4][:, :, None] - other[4][:, None, :]
                along = rel_x * delta_x + rel_y * delta_y
                jump = own[5][:, :, None] - other[5][:, None, :]
                mean_p = 0.5 * (own[5][:, :, None] + other[5][:, None, :])
                scaled = grad_mag * weight[:, None, :]
                total_rho = total_rho + lax.optimization_barrier(jnp.sum(scaled * (0.5 * along - jump * dist / (2.0 * sound_speed)), -1))
                star = mean_p - 0.5 * sound_speed * along / jnp.sqrt(dist_sq + regular_sq)
                force = scaled * star
                total_x = total_x + lax.optimization_barrier(jnp.sum(force * delta_x, -1))
                total_y = total_y + lax.optimization_barrier(jnp.sum(force * delta_y, -1))
        return jnp.stack([2.0 * own[2] * total_rho, -2.0 * total_x / own_rho, -2.0 * total_y / own_rho])
    result = lax.map(one_row, jnp.arange(rows, dtype=jnp.int32))
    return jnp.transpose(result, (1, 0, 2, 3))

def reference(offsets, density, velocity, counts, walls):
    occupied = (lax.broadcasted_iota(jnp.int32, density.shape, 2) < counts[:, :, None]).astype(jnp.float32)
    occ_pad = jnp.pad(occupied, ((1, 1), (1, 1), (0, 0)))
    keep = (1 - walls).astype(jnp.float32)[None, :, :, None]
    gravity = jnp.array([0.0, -gravity_accel], jnp.float32)[:, None, None, None]
    positions = offsets
    dens_now = density
    vel_now = velocity * keep
    for substep in range(ITERS):
        pressure = stiffness * (dens_now - 1.0)
        speed = jnp.sqrt(vel_now[0] * vel_now[0] + vel_now[1] * vel_now[1])
        top_speed = jnp.max(sound_speed + occupied * speed)
        step_size = courant * smoothing / top_speed
        stacked = jnp.concatenate([positions, dens_now[None], vel_now, pressure[None]], 0)
        padded = jnp.pad(stacked, ((0, 0), (1, 1), (1, 1), (0, 0)))
        rates = pair_rates(padded, occ_pad)
        dens_now = dens_now + step_size * occupied * rates[0]
        vel_now = (vel_now + step_size * occupied[None] * (rates[1:3] + gravity)) * keep
        positions = positions + step_size * occupied[None] * vel_now
    return (positions, dens_now, vel_now)
```

```python
import functools
import math

import jax
import jax.numpy as jnp
from jax import lax
from jax.experimental import pallas as pl
from jax.experimental.pallas import tpu as pltpu
from jax.sharding import PartitionSpec as P

ITERS = 3
ROWS = 2
COLS = 16
SLOTS = 128
FIELDS = 8
BLOCK = 16
MESH = pl.DeviceIdType.MESH

courant = 0.2
smoothing = 0.1625
gravity_accel = 9.81
kernel_norm = 7.0 / (4.0 * math.pi * smoothing * smoothing)
grad_coef = -5.0 * kernel_norm / (smoothing * smoothing)
unit = 1.0 / (2.0 * smoothing)
rho_coef = 2.0 * grad_coef * smoothing
vel_coef = -2.0 * grad_coef * 2.0 * smoothing * 5.0
SIDES = tuple((a, b) for a in (-1, 0, 1) for b in (-1, 0, 1) if (a, b) != (0, 0))


def column(row):
    wide = jnp.broadcast_to(row, (COLS, COLS))
    r = lax.broadcasted_iota(jnp.int32, (COLS, COLS), 0)
    c = lax.broadcasted_iota(jnp.int32, (COLS, COLS), 1)
    return jnp.sum(jnp.where(r == c, wide, 0.0), axis=1, keepdims=True)


def pair_terms(own, other, totals):
    xi, yi, vxi, vyi, ppi = own
    xj, yj, vxj, vyj, ppj, wj = other
    ux = xi - xj
    uy = yi - yj
    u2 = ux * ux + uy * uy
    length = u2 * lax.rsqrt(jnp.maximum(u2, 1e-30))
    soft = lax.rsqrt(u2 + 0.0025)
    support = jnp.maximum(1.0 - length, 0.0)
    grad = (support * support) * (support * wj)
    along = (vxi - vxj) * ux + (vyi - vyj) * uy
    force = grad * ((ppi + ppj) - along * soft)
    return (
        totals[0] + grad * (along - (ppi - ppj) * length),
        totals[1] + force * ux,
        totals[2] + force * uy,
    )


def kernel(
    off, den, vel, cnt, wal, o_off, o_den, o_vel,
    field, own_t, rate_t, occ_ref, keep_ref, msg_a, msg_b, slot_a, slot_b,
    halo_send, halo_recv, a_send, a_recv, b_send, b_recv,
):
    gx = lax.axis_index("gx")
    gy = lax.axis_index("gy")
    n_gx = lax.axis_size("gx")
    n_gy = lax.axis_size("gy")
    core = lax.rem(gy, 2)
    plane = lax.div(gy, 2)
    n_plane = n_gy // 2

    def side(a, b):
        return {"gx": lax.rem(gx + a + n_gx, n_gx), "gy": lax.rem(gy + b + n_gy, n_gy)}

    def peer_a(k):
        return {"gx": lax.rem(gx + k // 2, n_gx), "gy": plane * 2 + (lax.rem(core + 1, 2) if k % 2 else core)}

    def peer_b(k):
        return {"gx": gx, "gy": lax.rem(plane + k, n_plane) * 2 + core}

    peers_a = [peer_a(k) for k in range(1, 2 * n_gx)]
    peers_b = [peer_b(k) for k in range(1, n_plane)]
    sides = [side(a, b) for a, b in SIDES]

    barrier = pltpu.get_barrier_semaphore()
    for target in peers_a + peers_b + sides:
        pl.semaphore_signal(barrier, inc=1, device_id=target, device_id_type=MESH)

    lane = lax.broadcasted_iota(jnp.int32, (COLS, SLOTS), 1)
    for a in range(ROWS):
        occ = (lane.astype(jnp.float32) < column(cnt[a : a + 1, :].astype(jnp.float32))).astype(jnp.float32)
        keep = jnp.broadcast_to(column(1.0 - wal[a : a + 1, :].astype(jnp.float32)), (COLS, SLOTS))
        occ_ref[a] = occ
        keep_ref[a] = keep
        for c in range(2):
            o_off[c, a] = off[c, a]
            o_vel[c, a] = vel[c, a] * keep
        o_den[a] = den[a]

    def publish(s):
        best = jnp.zeros((COLS, SLOTS), jnp.float32)
        for a in range(ROWS):
            occ = occ_ref[a]
            rho = o_den[a]
            vx = o_vel[0, a]
            vy = o_vel[1, a]
            best = jnp.maximum(best, occ * (vx * vx + vy * vy))
            rows = [
                o_off[0, a] * unit,
                o_off[1, a] * unit,
                vx,
                vy,
                10.0 * (rho - 1.0),
                occ / (64.0 * (rho + 1.0 - occ)),
                occ,
                jnp.zeros_like(occ),
            ]
            for f in range(FIELDS):
                for b in range(COLS):
                    field[s, a + 1, b + 1, f : f + 1, :] = rows[f][b : b + 1]
            own_t[a] = jnp.concatenate(rows, 0).T
        msg_a[s] = jnp.broadcast_to(jnp.max(best, keepdims=True).reshape(1, 1), (1, SLOTS))

    def halo(s):
        copies = []
        for k, (a, b) in enumerate(SIDES):
            src_r = pl.ds(1, 2) if a == 0 else (1 if a < 0 else 2)
            dst_r = pl.ds(1, 2) if a == 0 else (3 if a < 0 else 0)
            src_c = pl.ds(1, COLS) if b == 0 else (1 if b < 0 else COLS)
            dst_c = pl.ds(1, COLS) if b == 0 else (COLS + 1 if b < 0 else 0)
            copies.append(
                pltpu.make_async_remote_copy(
                    src_ref=field.at[s, src_r, src_c],
                    dst_ref=field.at[s, dst_r, dst_c],
                    send_sem=halo_send.at[s, k],
                    recv_sem=halo_recv.at[s, k],
                    device_id=sides[k],
                    device_id_type=MESH,
                )
            )
        return copies

    def spread(s, peers, msg, slots, me, send, recv):
        slots[s, me] = msg[s]
        for target in peers:
            pltpu.make_async_remote_copy(
                src_ref=msg.at[s], dst_ref=slots.at[s, me], send_sem=send.at[s], recv_sem=recv.at[s],
                device_id=target, device_id_type=MESH,
            ).start()

    def gathered(s, peers, slots, send, recv):
        n = len(peers)
        whole = slots.at[s, pl.ds(0, n)]
        return pltpu.make_async_remote_copy(
            src_ref=whole, dst_ref=whole, send_sem=send.at[s], recv_sem=recv.at[s],
            device_id=peers[0], device_id_type=MESH,
        )

    def clear_outside(s):
        zeros_row = jnp.zeros((COLS + 2, FIELDS, SLOTS), jnp.float32)
        zeros_col = jnp.zeros((ROWS + 2, 1, FIELDS, SLOTS), jnp.float32)

        @pl.when(gx == 0)
        def _():
            field[s, 0] = zeros_row

        @pl.when(gx == n_gx - 1)
        def _():
            field[s, ROWS + 1] = zeros_row

        @pl.when(gy == 0)
        def _():
            field[s, :, 0:1] = zeros_col

        @pl.when(gy == n_gy - 1)
        def _():
            field[s, :, COLS + 1 : COLS + 2] = zeros_col

    lanes = lax.broadcasted_iota(jnp.int32, (BLOCK, SLOTS), 1)
    zeros = jnp.zeros((BLOCK, SLOTS), jnp.float32)

    def dense(s):
        def tile(t, carry):
            a = lax.div(t, SLOTS // BLOCK)
            i0 = pl.multiple_of(lax.rem(t, SLOTS // BLOCK) * BLOCK, BLOCK)
            mine = own_t[a, pl.ds(i0, BLOCK), :]

            def cell(b, rates):
                turned = pltpu.roll(mine, lax.rem(SLOTS - b, SLOTS), 1)
                own = [jnp.broadcast_to(turned[:, COLS * f : COLS * f + 1], (BLOCK, SLOTS)) for f in range(5)]
                totals = (zeros, zeros, zeros)
                for da in range(3):
                    for db in range(3):
                        rows = [field[s, a + da, b + db, f : f + 1, :] for f in range(6)]
                        rows[0] = rows[0] + (da - 1) * unit
                        rows[1] = rows[1] + (db - 1) * unit
                        totals = pair_terms(own, rows, totals)
                for f in range(3):
                    rates = jnp.where(lanes == f * COLS + b, jnp.sum(totals[f], 1, keepdims=True), rates)
                return rates

            rate_t[a, pl.ds(i0, BLOCK), :] = lax.fori_loop(0, COLS, cell, zeros)
            return carry

        lax.fori_loop(0, ROWS * SLOTS // BLOCK, tile, 0)

    def update(s, step):
        for a in range(ROWS):
            rates = rate_t[a].T
            occ = occ_ref[a]
            keep = keep_ref[a]
            rho = o_den[a]
            gain = step * occ
            scale = vel_coef / (rho + 1.0 - occ)
            o_den[a] = rho + gain * (rho_coef * rho * rates[0:COLS])
            vx = (o_vel[0, a] + gain * (scale * rates[COLS : 2 * COLS])) * keep
            vy = (o_vel[1, a] + gain * (scale * rates[2 * COLS : 3 * COLS] - gravity_accel)) * keep
            o_vel[0, a] = vx
            o_vel[1, a] = vy
            o_off[0, a] = o_off[0, a] + gain * vx
            o_off[1, a] = o_off[1, a] + gain * vy

    me_a = gx * 2 + core
    me_b = plane
    for s in range(ITERS):
        publish(s)
        if s == 0:
            pl.semaphore_wait(barrier, len(peers_a) + len(peers_b) + len(sides))
        copies = halo(s)
        for copy in copies:
            copy.start()
        spread(s, peers_a, msg_a, slot_a, me_a, a_send, a_recv)
        for copy in copies:
            copy.wait_recv()
        clear_outside(s)
        gathered(s, peers_a, slot_a, a_send, a_recv).wait_recv()
        msg_b[s] = jnp.max(slot_a[s], axis=0)
        spread(s, peers_b, msg_b, slot_b, me_b, b_send, b_recv)
        dense(s)
        gathered(s, peers_b, slot_b, b_send, b_recv).wait_recv()
        top = 10.0 + jnp.sqrt(jnp.max(slot_b[s], axis=0))
        update(s, courant * smoothing / top)
        for copy in copies:
            copy.wait_send()
        gathered(s, peers_a, slot_a, a_send, a_recv).wait_send()
        gathered(s, peers_b, slot_b, b_send, b_recv).wait_send()


def shards(n_gx, n_gy, offsets, density, velocity, counts, walls):
    shape = jax.ShapeDtypeStruct
    dma = pltpu.SemaphoreType.DMA
    f32 = jnp.float32
    n_a, n_b = 2 * n_gx, n_gy // 2
    return pl.pallas_call(
        kernel,
        out_shape=(shape(offsets.shape, f32), shape(density.shape, f32), shape(velocity.shape, f32)),
        in_specs=[pl.BlockSpec(memory_space=pltpu.VMEM)] * 5,
        out_specs=tuple(pl.BlockSpec(memory_space=pltpu.VMEM) for _ in range(3)),
        scratch_shapes=[
            pltpu.VMEM((ITERS, ROWS + 2, COLS + 2, FIELDS, SLOTS), f32),
            pltpu.VMEM((ROWS, SLOTS, SLOTS), f32),
            pltpu.VMEM((ROWS, SLOTS, SLOTS), f32),
            pltpu.VMEM((ROWS, COLS, SLOTS), f32),
            pltpu.VMEM((ROWS, COLS, SLOTS), f32),
            pltpu.VMEM((ITERS, 1, SLOTS), f32),
            pltpu.VMEM((ITERS, 1, SLOTS), f32),
            pltpu.VMEM((ITERS, n_a, 1, SLOTS), f32),
            pltpu.VMEM((ITERS, n_b, 1, SLOTS), f32),
            dma((ITERS, 8)),
            dma((ITERS, 8)),
            dma((ITERS,)),
            dma((ITERS,)),
            dma((ITERS,)),
            dma((ITERS,)),
        ],
        compiler_params=pltpu.CompilerParams(collective_id=0, has_side_effects=True),
    )(offsets, density, velocity, counts, walls)


def solution(mesh):
    fields = P(None, "gx", "gy", None)
    cells = P("gx", "gy")
    return jax.shard_map(
        functools.partial(shards, mesh.shape["gx"], mesh.shape["gy"]),
        mesh=mesh,
        in_specs=(fields, P("gx", "gy", None), fields, cells, cells),
        out_specs=(fields, P("gx", "gy", None), fields),
        check_vma=False,
    )
```

```python
import functools
import math

import jax
import jax.numpy as jnp
from jax import lax
from jax.experimental import pallas as pl
from jax.experimental.pallas import tpu as pltpu
from jax.sharding import PartitionSpec as P

ITERS = 3
ROWS = 2
COLS = 16
SLOTS = 128
FIELDS = 8
BLOCK = 16
OWN_FIELDS = 5
CELLS = ROWS * COLS
PAIRS = CELLS // 2
RING = 2
MESH = pl.DeviceIdType.MESH

courant = 0.2
smoothing = 0.1625
gravity_accel = 9.81
kernel_norm = 7.0 / (4.0 * math.pi * smoothing * smoothing)
grad_coef = -5.0 * kernel_norm / (smoothing * smoothing)
unit = 1.0 / (2.0 * smoothing)
rho_coef = 2.0 * grad_coef * smoothing
vel_coef = -2.0 * grad_coef * 2.0 * smoothing * 5.0
longest = 2.0 * courant * smoothing / 10.0
margin = 0.01
SIDES = tuple((a, b) for a in (-1, 0, 1) for b in (-1, 0, 1) if (a, b) != (0, 0))


def column(row):
    wide = jnp.broadcast_to(row, (COLS, COLS))
    r = lax.broadcasted_iota(jnp.int32, (COLS, COLS), 0)
    c = lax.broadcasted_iota(jnp.int32, (COLS, COLS), 1)
    return jnp.sum(jnp.where(r == c, wide, 0.0), axis=1, keepdims=True)


def pair_terms(own, other, totals):
    xi, yi, vxi, vyi, ppi = own
    xj, yj, vxj, vyj, ppj, wj = other
    ux = xi - xj
    uy = yi - yj
    u2 = ux * ux + uy * uy
    length = u2 * lax.rsqrt(jnp.maximum(u2, 1e-30))
    soft = lax.rsqrt(u2 + 0.0025)
    support = jnp.maximum(1.0 - length, 0.0)
    grad = (support * support) * (support * wj)
    along = (vxi - vxj) * ux + (vyi - vyj) * uy
    force = grad * ((ppi + ppj) - along * soft)
    return (
        totals[0] + grad * (along - (ppi - ppj) * length),
        totals[1] + force * ux,
        totals[2] + force * uy,
    )


def pieces(x):
    high = x.astype(jnp.bfloat16).astype(jnp.float32)
    rest = x - high
    middle = rest.astype(jnp.bfloat16).astype(jnp.float32)
    return high, middle, rest - middle


def kernel(
    ring, off, den, vel, cnt, wal, o_off, o_den, o_vel, o_flag,
    field, rate_t, occ_ref, keep_ref, msg_a, msg_b, slot_a, slot_b,
    halo_send, halo_recv, a_send, a_recv, b_send, b_recv, *extra,
):
    f32 = jnp.float32
    if ring:
        own_p, pick, bc0, bc1, acc0, acc1, ring0, ring1, code, natural, ranks, box_lo, box_hi, bad = extra
        bcs, accs, rings = (bc0, bc1), (acc0, acc1), (ring0, ring1)
    else:
        (own_t,) = extra
    gx = lax.axis_index("gx")
    gy = lax.axis_index("gy")
    n_gx = lax.axis_size("gx")
    n_gy = lax.axis_size("gy")
    core = lax.rem(gy, 2)
    plane = lax.div(gy, 2)
    n_plane = n_gy // 2

    def side(a, b):
        return {"gx": lax.rem(gx + a + n_gx, n_gx), "gy": lax.rem(gy + b + n_gy, n_gy)}

    def peer_a(k):
        return {"gx": lax.rem(gx + k // 2, n_gx), "gy": plane * 2 + (lax.rem(core + 1, 2) if k % 2 else core)}

    def peer_b(k):
        return {"gx": gx, "gy": lax.rem(plane + k, n_plane) * 2 + core}

    peers_a = [peer_a(k) for k in range(1, 2 * n_gx)]
    peers_b = [peer_b(k) for k in range(1, n_plane)]
    sides = [side(a, b) for a, b in SIDES]

    barrier = pltpu.get_barrier_semaphore()
    for target in peers_a + peers_b + sides:
        pl.semaphore_signal(barrier, inc=1, device_id=target, device_id_type=MESH)

    lane = lax.broadcasted_iota(jnp.int32, (COLS, SLOTS), 1)
    lane_row = lax.broadcasted_iota(jnp.int32, (1, SLOTS), 1)
    for a in range(ROWS):
        occ = (lane.astype(f32) < column(cnt[a : a + 1, :].astype(f32))).astype(f32)
        keep = jnp.broadcast_to(column(1.0 - wal[a : a + 1, :].astype(f32)), (COLS, SLOTS))
        occ_ref[a] = occ
        keep_ref[a] = keep
        for c in range(2):
            o_off[c, a] = off[c, a]
            o_vel[c, a] = vel[c, a] * keep
        o_den[a] = den[a]
    rate_t[...] = jnp.zeros_like(rate_t)
    if ring:
        bad[...] = jnp.zeros_like(bad)
        r = lax.broadcasted_iota(jnp.int32, pick.shape, 0)
        c = lax.broadcasted_iota(jnp.int32, pick.shape, 1)
        group = r // COLS
        hit = (group % OWN_FIELDS == c // SLOTS) & (group < 3 * OWN_FIELDS)
        pick[...] = jnp.where(hit, 1.0, 0.0).astype(jnp.bfloat16)

    def fastest(s):
        best = jnp.zeros((COLS, SLOTS), f32)
        for a in range(ROWS):
            vx = o_vel[0, a]
            vy = o_vel[1, a]
            best = jnp.maximum(best, occ_ref[a] * (vx * vx + vy * vy))
        best = jnp.max(best, keepdims=True).reshape(1, 1)
        if ring:
            msg_a[s] = jnp.where(lane_row < SLOTS // 2, best, jnp.max(bad[...], keepdims=True).reshape(1, 1))
        else:
            msg_a[s] = jnp.broadcast_to(best, (1, SLOTS))

    def publish(s):
        for a in range(ROWS):
            occ = occ_ref[a]
            rho = o_den[a]
            rows = [
                o_off[0, a] * unit,
                o_off[1, a] * unit,
                o_vel[0, a],
                o_vel[1, a],
                10.0 * (rho - 1.0),
                occ / (64.0 * (rho + 1.0 - occ)),
                occ,
                jnp.zeros_like(occ),
            ]
            for f in range(FIELDS):
                for b in range(COLS):
                    field[s, a + 1, b + 1, f : f + 1, :] = rows[f][b : b + 1]
            if not ring:
                own_t[a] = jnp.concatenate(rows, 0).T

    def turn():
        for a in range(ROWS):
            rows = [
                o_off[0, a] * unit, o_off[1, a] * unit, o_vel[0, a], o_vel[1, a], 10.0 * (o_den[a] - 1.0),
            ]
            parts = [pieces(x) for x in rows]
            flat = [p[n] for n in range(3) for p in parts] + [jnp.zeros((COLS, SLOTS), f32)]
            for n in range(2):
                half = jnp.concatenate(flat[8 * n : 8 * n + 8], 0)
                own_p[a, :, n * SLOTS : (n + 1) * SLOTS] = half.T.astype(jnp.bfloat16)

    def halo(s):
        copies = []
        for k, (a, b) in enumerate(SIDES):
            src_r = pl.ds(1, 2) if a == 0 else (1 if a < 0 else 2)
            dst_r = pl.ds(1, 2) if a == 0 else (3 if a < 0 else 0)
            src_c = pl.ds(1, COLS) if b == 0 else (1 if b < 0 else COLS)
            dst_c = pl.ds(1, COLS) if b == 0 else (COLS + 1 if b < 0 else 0)
            copies.append(
                pltpu.make_async_remote_copy(
                    src_ref=field.at[s, src_r, src_c],
                    dst_ref=field.at[s, dst_r, dst_c],
                    send_sem=halo_send.at[s, k],
                    recv_sem=halo_recv.at[s, k],
                    device_id=sides[k],
                    device_id_type=MESH,
                )
            )
        return copies

    def spread(s, peers, msg, slots, me, send, recv):
        slots[s, me] = msg[s]
        for target in peers:
            pltpu.make_async_remote_copy(
                src_ref=msg.at[s], dst_ref=slots.at[s, me], send_sem=send.at[s], recv_sem=recv.at[s],
                device_id=target, device_id_type=MESH,
            ).start()

    def gathered(s, peers, slots, send, recv):
        n = len(peers)
        whole = slots.at[s, pl.ds(0, n)]
        return pltpu.make_async_remote_copy(
            src_ref=whole, dst_ref=whole, send_sem=send.at[s], recv_sem=recv.at[s],
            device_id=peers[0], device_id_type=MESH,
        )

    def clear_outside(s):
        zeros_row = jnp.zeros((COLS + 2, FIELDS, SLOTS), f32)
        zeros_col = jnp.zeros((ROWS + 2, 1, FIELDS, SLOTS), f32)

        @pl.when(gx == 0)
        def _():
            field[s, 0] = zeros_row

        @pl.when(gx == n_gx - 1)
        def _():
            field[s, ROWS + 1] = zeros_row

        @pl.when(gy == 0)
        def _():
            field[s, :, 0:1] = zeros_col

        @pl.when(gy == n_gy - 1)
        def _():
            field[s, :, COLS + 1 : COLS + 2] = zeros_col

    lanes = lax.broadcasted_iota(jnp.int32, (BLOCK, SLOTS), 1)
    zeros = jnp.zeros((BLOCK, SLOTS), f32)

    def dense(s):
        def tile(t, carry):
            a = lax.div(t, SLOTS // BLOCK)
            i0 = pl.multiple_of(lax.rem(t, SLOTS // BLOCK) * BLOCK, BLOCK)
            mine = own_t[a, pl.ds(i0, BLOCK), :]

            def cell(b, rates):
                turned = pltpu.roll(mine, lax.rem(SLOTS - b, SLOTS), 1)
                own = [jnp.broadcast_to(turned[:, COLS * f : COLS * f + 1], (BLOCK, SLOTS)) for f in range(5)]
                totals = (zeros, zeros, zeros)
                for da in range(3):
                    for db in range(3):
                        rows = [field[s, a + da, b + db, f : f + 1, :] for f in range(6)]
                        rows[0] = rows[0] + (da - 1) * unit
                        rows[1] = rows[1] + (db - 1) * unit
                        totals = pair_terms(own, rows, totals)
                for f in range(3):
                    rates = jnp.where(lanes == f * COLS + b, jnp.sum(totals[f], 1, keepdims=True), rates)
                return rates

            rate_t[a, pl.ds(i0, BLOCK), :] = lax.fori_loop(0, COLS, cell, zeros)
            return carry

        lax.fori_loop(0, ROWS * SLOTS // BLOCK, tile, 0)

    def boxes():
        for a in range(ROWS):
            for d in range(2):
                x = o_off[d, a] * unit
                way = o_vel[d, a] * (longest * unit)
                box_lo[d, a] = x + jnp.minimum(way, 0.0) - margin * unit
                box_hi[d, a] = x + jnp.maximum(way, 0.0) + margin * unit

    def check():
        for a in range(ROWS):
            inside = occ_ref[a] < 0.5
            both = None
            for d in range(2):
                x = o_off[d, a] * unit
                within = (x >= box_lo[d, a]) & (x <= box_hi[d, a])
                both = within if both is None else both & within
            bad[...] = jnp.maximum(bad[...], jnp.where(inside | both, 0.0, 1.0))

    def lists():
        def copy_row(t, carry):
            r = lax.div(t, COLS + 2)
            c = lax.rem(t, COLS + 2)
            for n, f in enumerate((0, 1, 2, 3, 6)):
                natural[n, r, pl.ds(c, 1), :] = field[0, r, c, f : f + 1, :]
            return carry

        lax.fori_loop(0, (ROWS + 2) * (COLS + 2), copy_row, 0)
        reach = 1.0001
        masks = []
        for k, (da, db) in enumerate(SIDES):
            for a in range(ROWS):
                there = [natural[n, a + 1 + da, 1 + db : 1 + db + COLS, :] for n in range(5)]
                near = there[4] > 0.5
                for d, shift in ((0, da), (1, db)):
                    occ = occ_ref[a] > 0.5
                    low = jnp.min(jnp.where(occ, box_lo[d, a], 1e30), axis=1, keepdims=True) - reach
                    high = jnp.max(jnp.where(occ, box_hi[d, a], -1e30), axis=1, keepdims=True) + reach
                    x = there[d] + shift * unit
                    way = there[2 + d] * (longest * unit)
                    near = near & (x + jnp.maximum(way, 0.0) + margin * unit > low)
                    near = near & (x + jnp.minimum(way, 0.0) - margin * unit < high)
                masks.append(jnp.where(near, 1.0, 0.0))
        r = lax.broadcasted_iota(jnp.int32, (SLOTS, SLOTS), 0)
        c = lax.broadcasted_iota(jnp.int32, (SLOTS, SLOTS), 1)
        upper = jnp.where(r <= c, 1.0, 0.0).astype(jnp.bfloat16)
        stacked = jnp.concatenate(masks, 0).astype(jnp.bfloat16)
        ranks[...] = jnp.dot(stacked, upper, preferred_element_type=f32).astype(jnp.int32)
        where_to = lax.broadcasted_iota(jnp.int32, (8, SLOTS), 1)
        for g in range(CELLS // 8):
            base = jnp.zeros((8, 1), jnp.int32)
            for k in range(8):
                table = ranks[(k * CELLS + 8 * g) : (k * CELLS + 8 * g + 8), :]
                count = table[:, SLOTS - 1 : SLOTS]
                for t in range(RING):
                    rank = where_to + (SLOTS * t + 1) - base
                    spot = jnp.zeros((8, SLOTS), jnp.int32)
                    for bit in (64, 32, 16, 8, 4, 2, 1):
                        probe = jnp.take_along_axis(table, spot + (bit - 1), axis=1)
                        spot = jnp.where(probe < rank, spot + bit, spot)
                    code[t, k, 8 * g : 8 * g + 8, :] = jnp.where((rank >= 1) & (rank <= count), spot, -1)
                base = base + count
            over = jnp.where(base > RING * SLOTS, 1.0, 0.0)
            bad[0:8, :] = jnp.maximum(bad[0:8, :], jnp.broadcast_to(over, (8, SLOTS)))

    field_row = lax.broadcasted_iota(jnp.int32, (FIELDS, SLOTS), 0)

    def broadcast_own(c, dst):
        a = lax.div(c, COLS)
        b = lax.rem(c, COLS)
        mine = own_p[a]
        at = lax.broadcasted_iota(jnp.int32, mine.shape, 1) % COLS
        mine = jnp.where(at == b, mine.astype(f32), 0.0).astype(jnp.bfloat16)
        wide = jnp.dot(mine, pick[...], preferred_element_type=f32)
        for f in range(OWN_FIELDS):
            dst[f] = wide[:, f * SLOTS : (f + 1) * SLOTS]

    def sweep(bc, acc, tiles, first):
        for i0 in range(0, SLOTS, BLOCK):
            here = pl.ds(i0, BLOCK)
            own = [bc[f, here, :] for f in range(OWN_FIELDS)]
            totals = (zeros, zeros, zeros) if first else tuple(acc[f, here, :] for f in range(3))
            for rows in tiles:
                totals = pair_terms(own, rows, totals)
            for f in range(3):
                acc[f, here, :] = totals[f]

    def own_pass(s):
        broadcast_own(0, bc0.at[0])

        def two(u, carry):
            for n in range(2):
                c = 2 * u + n
                a = lax.div(c, COLS)
                b = lax.rem(c, COLS)
                later = jnp.minimum(c + 1, CELLS - 1)
                broadcast_own(later, bcs[1 - n].at[u + n])
                rows = [field[s, a + 1, b + 1, f : f + 1, :] for f in range(6)]
                sweep(bcs[n].at[u], accs[n].at[u], [rows], True)
            return carry

        lax.fori_loop(0, PAIRS, two, 0)

    def pack(s, c, dst):
        a = lax.div(c, COLS)
        b = lax.rem(c, COLS)
        for t in range(RING):
            packed = jnp.zeros((FIELDS, SLOTS), f32)
            for k, (da, db) in enumerate(SIDES):
                take = jnp.broadcast_to(code[t, k, pl.ds(c, 1), :], (FIELDS, SLOTS))
                moved = jnp.take_along_axis(field[s, a + 1 + da, b + 1 + db], take & (SLOTS - 1), axis=1)
                shift = jnp.where(field_row == 0, da * unit, jnp.where(field_row == 1, db * unit, 0.0))
                packed = jnp.where(take >= 0, moved + shift, packed)
            dst[t] = packed

    def collect(c, acc, valid):
        a = lax.div(c, COLS)
        b = lax.rem(c, COLS)
        if valid is not None:
            b = jnp.where(valid, b, -4 * SLOTS)
        for i0 in range(0, SLOTS, BLOCK):
            here = pl.ds(i0, BLOCK)
            rates = rate_t[a, here, :]
            for f in range(3):
                rates = jnp.where(lanes == f * COLS + b, jnp.sum(acc[f, here, :], 1, keepdims=True), rates)
            rate_t[a, here, :] = rates

    def ring_pass(s):
        for n in range(2):
            pack(s, n, rings[n].at[0])

        def two(u, carry):
            for n in range(2):
                c = 2 * u + n
                if n == 0:
                    collect(jnp.maximum(c - 1, 0), acc1.at[jnp.maximum(u - 1, 0)], c > 0)
                else:
                    collect(c - 1, acc0.at[u], None)
                tiles = [[rings[n][u, t, f : f + 1, :] for f in range(6)] for t in range(RING)]
                sweep(bcs[n].at[u], accs[n].at[u], tiles, False)
                pack(s, jnp.minimum(c + 2, CELLS - 1), rings[n].at[u + 1])
            return carry

        lax.fori_loop(0, PAIRS, two, 0)
        collect(CELLS - 1, acc1.at[PAIRS - 1], None)

    def update(s, step):
        for a in range(ROWS):
            rates = rate_t[a].T
            occ = occ_ref[a]
            keep = keep_ref[a]
            rho = o_den[a]
            gain = step * occ
            scale = vel_coef / (rho + 1.0 - occ)
            o_den[a] = rho + gain * (rho_coef * rho * rates[0:COLS])
            vx = (o_vel[0, a] + gain * (scale * rates[COLS : 2 * COLS])) * keep
            vy = (o_vel[1, a] + gain * (scale * rates[2 * COLS : 3 * COLS] - gravity_accel)) * keep
            o_vel[0, a] = vx
            o_vel[1, a] = vy
            o_off[0, a] = o_off[0, a] + gain * vx
            o_off[1, a] = o_off[1, a] + gain * vy

    me_a = gx * 2 + core
    me_b = plane
    for s in range(ITERS):
        fastest(s)
        if s == 0:
            pl.semaphore_wait(barrier, len(peers_a) + len(peers_b) + len(sides))
        spread(s, peers_a, msg_a, slot_a, me_a, a_send, a_recv)
        publish(s)
        copies = halo(s)
        for copy in copies:
            copy.start()
        if ring:
            if s == 0:
                boxes()
            turn()
            own_pass(s)
        gathered(s, peers_a, slot_a, a_send, a_recv).wait_recv()
        msg_b[s] = jnp.max(slot_a[s], axis=0)
        spread(s, peers_b, msg_b, slot_b, me_b, b_send, b_recv)
        for copy in copies:
            copy.wait_recv()
        clear_outside(s)
        if ring:
            if s == 0:
                lists()
            ring_pass(s)
        else:
            dense(s)
        gathered(s, peers_b, slot_b, b_send, b_recv).wait_recv()
        result = jnp.max(slot_b[s], axis=0)
        top = 10.0 + jnp.sqrt(result[:, 0:1])
        update(s, courant * smoothing / top)
        if ring and s < ITERS - 1:
            check()
        for copy in copies:
            copy.wait_send()
        gathered(s, peers_a, slot_a, a_send, a_recv).wait_send()
        gathered(s, peers_b, slot_b, b_send, b_recv).wait_send()
    o_flag[...] = result


def substeps(ring, n_gx, n_gy, offsets, density, velocity, counts, walls):
    shape = jax.ShapeDtypeStruct
    dma = pltpu.SemaphoreType.DMA
    f32 = jnp.float32
    n_a, n_b = 2 * n_gx, n_gy // 2
    if ring:
        extra = [
            pltpu.VMEM((ROWS, SLOTS, 2 * SLOTS), jnp.bfloat16),
            pltpu.VMEM((2 * SLOTS, OWN_FIELDS * SLOTS), jnp.bfloat16),
            pltpu.VMEM((PAIRS + 1, OWN_FIELDS, SLOTS, SLOTS), f32),
            pltpu.VMEM((PAIRS + 1, OWN_FIELDS, SLOTS, SLOTS), f32),
            pltpu.VMEM((PAIRS, 3, SLOTS, SLOTS), f32),
            pltpu.VMEM((PAIRS, 3, SLOTS, SLOTS), f32),
            pltpu.VMEM((PAIRS + 1, RING, FIELDS, SLOTS), f32),
            pltpu.VMEM((PAIRS + 1, RING, FIELDS, SLOTS), f32),
            pltpu.VMEM((RING, 8, CELLS, SLOTS), jnp.int32),
            pltpu.VMEM((5, ROWS + 2, 24, SLOTS), f32),
            pltpu.VMEM((8 * CELLS, SLOTS), jnp.int32),
            pltpu.VMEM((2, ROWS, COLS, SLOTS), f32),
            pltpu.VMEM((2, ROWS, COLS, SLOTS), f32),
            pltpu.VMEM((COLS, SLOTS), f32),
        ]
    else:
        extra = [pltpu.VMEM((ROWS, SLOTS, SLOTS), f32)]
    return pl.pallas_call(
        functools.partial(kernel, ring),
        out_shape=(
            shape(offsets.shape, f32),
            shape(density.shape, f32),
            shape(velocity.shape, f32),
            shape((1, SLOTS), f32),
        ),
        in_specs=[pl.BlockSpec(memory_space=pltpu.VMEM)] * 5,
        out_specs=tuple(pl.BlockSpec(memory_space=pltpu.VMEM) for _ in range(4)),
        scratch_shapes=[
            pltpu.VMEM((ITERS, ROWS + 2, COLS + 2, FIELDS, SLOTS), f32),
            pltpu.VMEM((ROWS, SLOTS, SLOTS), f32),
            pltpu.VMEM((ROWS, COLS, SLOTS), f32),
            pltpu.VMEM((ROWS, COLS, SLOTS), f32),
            pltpu.VMEM((ITERS, 1, SLOTS), f32),
            pltpu.VMEM((ITERS, 1, SLOTS), f32),
            pltpu.VMEM((ITERS, n_a, 1, SLOTS), f32),
            pltpu.VMEM((ITERS, n_b, 1, SLOTS), f32),
            dma((ITERS, 8)),
            dma((ITERS, 8)),
            dma((ITERS,)),
            dma((ITERS,)),
            dma((ITERS,)),
            dma((ITERS,)),
        ]
        + extra,
        compiler_params=pltpu.CompilerParams(collective_id=0 if ring else 1, has_side_effects=True),
    )(offsets, density, velocity, counts, walls)


def shards(n_gx, n_gy, *args):
    *fast, flag = substeps(True, n_gx, n_gy, *args)
    return lax.cond(
        flag[0, SLOTS - 1] > 0.0,
        lambda: tuple(substeps(False, n_gx, n_gy, *args)[:3]),
        lambda: tuple(fast),
    )


def solution(mesh):
    fields = P(None, "gx", "gy", None)
    cells = P("gx", "gy")
    return jax.shard_map(
        functools.partial(shards, mesh.shape["gx"], mesh.shape["gy"]),
        mesh=mesh,
        in_specs=(fields, P("gx", "gy", None), fields, cells, cells),
        out_specs=(fields, P("gx", "gy", None), fields),
        check_vma=False,
    )
```

```python
import functools
import math

import jax
import jax.numpy as jnp
from jax import lax
from jax.experimental import pallas as pl
from jax.experimental.pallas import tpu as pltpu
from jax.sharding import PartitionSpec as P

ITERS = 3
ROWS = 2
COLS = 16
SLOTS = 128
FIELDS = 8
BLOCK = 16
OWN_FIELDS = 5
CELLS = ROWS * COLS
WAYS = 2
TURNS = CELLS // WAYS
INNER = COLS - 2
INNER_TURNS = ROWS * INNER // WAYS
TILES = 2
LISTED = ((0, -1), (0, 1), (1, -1), (1, 0), (1, 1), (-1, -1), (-1, 0), (-1, 1))
NEAR = 5
PAST = tuple((k, 0 if LISTED[k][1] < 0 else COLS - 1) for k in range(NEAR) if LISTED[k][1] != 0)
MESH = pl.DeviceIdType.MESH

courant = 0.2
smoothing = 0.1625
gravity_accel = 9.81
kernel_norm = 7.0 / (4.0 * math.pi * smoothing * smoothing)
grad_coef = -5.0 * kernel_norm / (smoothing * smoothing)
unit = 1.0 / (2.0 * smoothing)
rho_coef = 2.0 * grad_coef * smoothing
vel_coef = -2.0 * grad_coef * 2.0 * smoothing * 5.0
longest = 2.0 * courant * smoothing / 10.0
margin = 0.01
SIDES = tuple((a, b) for a in (-1, 0, 1) for b in (-1, 0, 1) if (a, b) != (0, 0))


def column(row):
    wide = jnp.broadcast_to(row, (COLS, COLS))
    r = lax.broadcasted_iota(jnp.int32, (COLS, COLS), 0)
    c = lax.broadcasted_iota(jnp.int32, (COLS, COLS), 1)
    return jnp.sum(jnp.where(r == c, wide, 0.0), axis=1, keepdims=True)


def pair_terms(own, other, totals):
    xi, yi, vxi, vyi, ppi = own
    xj, yj, vxj, vyj, ppj, wj = other
    ux = xi - xj
    uy = yi - yj
    u2 = ux * ux + uy * uy
    length = u2 * lax.rsqrt(jnp.maximum(u2, 1e-30))
    soft = lax.rsqrt(u2 + 0.0025)
    support = jnp.maximum(1.0 - length, 0.0)
    grad = (support * support) * (support * wj)
    along = (vxi - vxj) * ux + (vyi - vyj) * uy
    force = grad * ((ppi + ppj) - along * soft)
    return (
        totals[0] + grad * (along - (ppi - ppj) * length),
        totals[1] + force * ux,
        totals[2] + force * uy,
    )


def lane_gather(x, index):
    return lax.gather(
        x,
        index[..., None],
        lax.GatherDimensionNumbers(
            offset_dims=(),
            collapsed_slice_dims=(1,),
            start_index_map=(1,),
            operand_batching_dims=(0,),
            start_indices_batching_dims=(0,),
        ),
        slice_sizes=(1, 1),
        mode=lax.GatherScatterMode.PROMISE_IN_BOUNDS,
    )


def pieces(x):
    high = x.astype(jnp.bfloat16).astype(jnp.float32)
    rest = x - high
    middle = rest.astype(jnp.bfloat16).astype(jnp.float32)
    return high, middle, rest - middle


def kernel(
    ring, off, den, vel, cnt, wal, o_off, o_den, o_vel, o_flag,
    field0, field1, field2, rate_t, occ_ref, keep_ref, msg_a, msg_b, slot_a, slot_b,
    halo_send, halo_recv, a_send, a_recv, b_send, b_recv, *extra,
):
    f32 = jnp.float32
    field = (field0, field1, field2)
    if ring:
        own_p, pick, code, natural, ranks, start, box_lo, box_hi, bad, *ways = extra
        bcs, accs, lates = [ways[WAYS * n : WAYS * (n + 1)] for n in range(3)]
    else:
        (own_t,) = extra
    gx = lax.axis_index("gx")
    gy = lax.axis_index("gy")
    n_gx = lax.axis_size("gx")
    n_gy = lax.axis_size("gy")
    core = lax.rem(gy, 2)
    plane = lax.div(gy, 2)
    n_plane = n_gy // 2

    def side(a, b):
        return {"gx": lax.rem(gx + a + n_gx, n_gx), "gy": lax.rem(gy + b + n_gy, n_gy)}

    def peer_a(k):
        return {"gx": lax.rem(gx + k // 2, n_gx), "gy": plane * 2 + (lax.rem(core + 1, 2) if k % 2 else core)}

    def peer_b(k):
        return {"gx": gx, "gy": lax.rem(plane + k, n_plane) * 2 + core}

    peers_a = [peer_a(k) for k in range(1, 2 * n_gx)]
    peers_b = [peer_b(k) for k in range(1, n_plane)]
    sides = [side(a, b) for a, b in SIDES]

    barrier = pltpu.get_barrier_semaphore()
    for target in peers_a + peers_b + sides:
        pl.semaphore_signal(barrier, inc=1, device_id=target, device_id_type=MESH)

    lane = lax.broadcasted_iota(jnp.int32, (COLS, SLOTS), 1)
    lane_row = lax.broadcasted_iota(jnp.int32, (1, SLOTS), 1)
    for a in range(ROWS):
        occ = (lane.astype(f32) < column(cnt[a : a + 1, :].astype(f32))).astype(f32)
        keep = jnp.broadcast_to(column(1.0 - wal[a : a + 1, :].astype(f32)), (COLS, SLOTS))
        occ_ref[a] = occ
        keep_ref[a] = keep
        for c in range(2):
            o_off[c, a] = off[c, a]
            o_vel[c, a] = vel[c, a] * keep
        o_den[a] = den[a]
    rate_t[...] = jnp.zeros_like(rate_t)
    for later in field[1:]:
        later[1 : ROWS + 1, 1 : COLS + 1] = jnp.zeros((ROWS, COLS, FIELDS, SLOTS), f32)
    if ring:
        bad[...] = jnp.zeros_like(bad)
        natural[...] = jnp.zeros_like(natural)
        r = lax.broadcasted_iota(jnp.int32, pick.shape, 0)
        c = lax.broadcasted_iota(jnp.int32, pick.shape, 1)
        group = r // 8
        hit = (group % OWN_FIELDS == c // SLOTS) & (group < 3 * OWN_FIELDS)
        pick[...] = jnp.where(hit, 1.0, 0.0).astype(jnp.bfloat16)

    def fastest(s):
        best = jnp.zeros((COLS, SLOTS), f32)
        for a in range(ROWS):
            vx = o_vel[0, a]
            vy = o_vel[1, a]
            best = jnp.maximum(best, occ_ref[a] * (vx * vx + vy * vy))
        best = jnp.max(best, keepdims=True).reshape(1, 1)
        if ring:
            msg_a[s] = jnp.where(lane_row < SLOTS // 2, best, jnp.max(bad[...], keepdims=True).reshape(1, 1))
        else:
            msg_a[s] = jnp.broadcast_to(best, (1, SLOTS))

    def publish(s):
        for a in range(ROWS):
            occ = occ_ref[a]
            rho = o_den[a]
            rows = [
                o_off[0, a] * unit,
                o_off[1, a] * unit,
                o_vel[0, a],
                o_vel[1, a],
                10.0 * (rho - 1.0),
                occ / (64.0 * (rho + 1.0 - occ)),
                occ,
                jnp.zeros_like(occ),
            ]
            for f in range(FIELDS if s == 0 else 6):
                for b in range(COLS):
                    field[s][a + 1, b + 1, f : f + 1, :] = rows[f][b : b + 1]
            if not ring:
                own_t[a] = jnp.concatenate(rows, 0).T

    def turn():
        for a in range(ROWS):
            rows = [o_off[0, a] * unit, o_off[1, a] * unit, o_vel[0, a], o_vel[1, a], 10.0 * (o_den[a] - 1.0)]
            parts = [pieces(x) for x in rows]
            for h in range(2):
                flat = [p[n][8 * h : 8 * h + 8] for n in range(3) for p in parts]
                flat.append(jnp.zeros((8, SLOTS), f32))
                own_p[2 * a + h] = jnp.concatenate(flat, 0).T.astype(jnp.bfloat16)

    def halo(s):
        copies = []
        for k, (a, b) in enumerate(SIDES):
            src_r = pl.ds(1, 2) if a == 0 else (1 if a < 0 else 2)
            dst_r = pl.ds(1, 2) if a == 0 else (3 if a < 0 else 0)
            src_c = pl.ds(1, COLS) if b == 0 else (1 if b < 0 else COLS)
            dst_c = pl.ds(1, COLS) if b == 0 else (COLS + 1 if b < 0 else 0)
            sent = slice(0, FIELDS if s == 0 else 6)
            copies.append(
                pltpu.make_async_remote_copy(
                    src_ref=field[s].at[src_r, src_c, sent],
                    dst_ref=field[s].at[dst_r, dst_c, sent],
                    send_sem=halo_send.at[s, k],
                    recv_sem=halo_recv.at[s, k],
                    device_id=sides[k],
                    device_id_type=MESH,
                )
            )
        return copies

    def spread(s, peers, msg, slots, me, send, recv):
        slots[s, me] = msg[s]
        for target in peers:
            pltpu.make_async_remote_copy(
                src_ref=msg.at[s], dst_ref=slots.at[s, me], send_sem=send.at[s], recv_sem=recv.at[s],
                device_id=target, device_id_type=MESH,
            ).start()

    def gathered(s, peers, slots, send, recv):
        n = len(peers)
        whole = slots.at[s, pl.ds(0, n)]
        return pltpu.make_async_remote_copy(
            src_ref=whole, dst_ref=whole, send_sem=send.at[s], recv_sem=recv.at[s],
            device_id=peers[0], device_id_type=MESH,
        )

    def clear_rows(s):
        empty = jnp.zeros((COLS, FIELDS, SLOTS), f32)

        @pl.when(gx == 0)
        def _():
            field[s][0, 1 : COLS + 1] = empty

        @pl.when(gx == n_gx - 1)
        def _():
            field[s][ROWS + 1, 1 : COLS + 1] = empty

    def clear_columns(s):
        empty = jnp.zeros((FIELDS, SLOTS), f32)
        for at, end in ((0, 0), (ROWS + 1, n_gx - 1)):

            @pl.when(gx == end)
            def _():
                field[s][at, 0] = empty
                field[s][at, COLS + 1] = empty

        for at, end in ((0, 0), (COLS + 1, n_gy - 1)):

            @pl.when(gy == end)
            def _():
                for r in range(ROWS + 2):
                    field[s][r, at] = empty

    lanes = lax.broadcasted_iota(jnp.int32, (BLOCK, SLOTS), 1)
    zeros = jnp.zeros((BLOCK, SLOTS), f32)

    def dense(s):
        def tile(t, carry):
            a = lax.div(t, SLOTS // BLOCK)
            i0 = pl.multiple_of(lax.rem(t, SLOTS // BLOCK) * BLOCK, BLOCK)
            mine = own_t[a, pl.ds(i0, BLOCK), :]

            def cell(b, rates):
                turned = pltpu.roll(mine, lax.rem(SLOTS - b, SLOTS), 1)
                own = [jnp.broadcast_to(turned[:, COLS * f : COLS * f + 1], (BLOCK, SLOTS)) for f in range(5)]
                totals = (zeros, zeros, zeros)
                for da in range(3):
                    for db in range(3):
                        rows = [field[s][a + da, b + db, f : f + 1, :] for f in range(6)]
                        rows[0] = rows[0] + (da - 1) * unit
                        rows[1] = rows[1] + (db - 1) * unit
                        totals = pair_terms(own, rows, totals)
                for f in range(3):
                    rates = jnp.where(lanes == f * COLS + b, jnp.sum(totals[f], 1, keepdims=True), rates)
                return rates

            rate_t[a, pl.ds(i0, BLOCK), :] = lax.fori_loop(0, COLS, cell, zeros)
            return carry

        lax.fori_loop(0, ROWS * SLOTS // BLOCK, tile, 0)

    def boxes():
        for a in range(ROWS):
            for d in range(2):
                x = o_off[d, a] * unit
                way = o_vel[d, a] * (longest * unit)
                box_lo[d, a] = x + jnp.minimum(way, 0.0) - margin * unit
                box_hi[d, a] = x + jnp.maximum(way, 0.0) + margin * unit

    def check():
        for a in range(ROWS):
            inside = occ_ref[a] < 0.5
            both = None
            for d in range(2):
                x = o_off[d, a] * unit
                within = (x >= box_lo[d, a]) & (x <= box_hi[d, a])
                both = within if both is None else both & within
            bad[...] = jnp.maximum(bad[...], jnp.where(inside | both, 0.0, 1.0))

    def near(there, low, high):
        hit = there[4] > 0.5
        for d in range(2):
            way = there[2 + d] * (longest * unit)
            hit = hit & (there[d] + jnp.maximum(way, 0.0) + margin * unit > low[d])
            hit = hit & (there[d] + jnp.minimum(way, 0.0) - margin * unit < high[d])
        return jnp.where(hit, 1.0, 0.0)

    def extents(a):
        occ = occ_ref[a] > 0.5
        reach = 1.0001
        low = [jnp.min(jnp.where(occ, box_lo[d, a], 1e30), axis=1, keepdims=True) - reach for d in range(2)]
        high = [jnp.max(jnp.where(occ, box_hi[d, a], -1e30), axis=1, keepdims=True) + reach for d in range(2)]
        return low, high

    def beside(a, k, rows):
        da = LISTED[k][0] * (1 - 2 * a)
        db = LISTED[k][1]
        there = [natural[n, a + 1 + da, 1 + db + rows.start : 1 + db + rows.stop, :] for n in range(5)]
        there[0] = there[0] + da * unit
        there[1] = there[1] + db * unit
        return there

    def count_up(masks, at):
        r = lax.broadcasted_iota(jnp.int32, (SLOTS, SLOTS), 0)
        c = lax.broadcasted_iota(jnp.int32, (SLOTS, SLOTS), 1)
        upper = jnp.where(r <= c, 1.0, 0.0).astype(jnp.bfloat16)
        stacked = jnp.concatenate(masks, 0).astype(jnp.bfloat16)
        ranks[at : at + stacked.shape[0], :] = jnp.dot(stacked, upper, preferred_element_type=f32).astype(jnp.int32)

    spread_lane = lax.broadcasted_iota(jnp.int32, (8, SLOTS), 1)

    def find(table, base, t):
        rank = spread_lane + (SLOTS * t + 1) - base
        spot = jnp.zeros((8, SLOTS), jnp.int32)
        for bit in (64, 32, 16, 8, 4, 2, 1):
            probe = lane_gather(table, spot + (bit - 1))
            spot = jnp.where(probe < rank, spot + bit, spot)
        return jnp.where((rank >= 1) & (rank <= table[:, SLOTS - 1 : SLOTS]), spot, -1)

    every = slice(0, COLS)

    def lists_near():
        for a in range(ROWS):
            whole = [o_off[0, a] * unit, o_off[1, a] * unit, o_vel[0, a], o_vel[1, a], occ_ref[a]]
            for n in range(5):
                natural[n, a + 1, 1 : COLS + 1, :] = whole[n]
        masks = []
        for a in range(ROWS):
            low, high = extents(a)
            masks += [near(beside(a, k, every), low, high) for k in range(NEAR)]
        count_up(masks, 0)
        for a in range(ROWS):
            for g in range(COLS // 8):
                rows = slice(a * COLS + 8 * g, a * COLS + 8 * g + 8)
                base = jnp.zeros((8, 1), jnp.int32)
                for k in range(NEAR):
                    at = (a * NEAR + k) * COLS + 8 * g
                    table = ranks[at : at + 8, :]
                    for t in range(TILES):
                        code[t, k, rows, :] = find(table, base, t)
                    base = base + table[:, SLOTS - 1 : SLOTS]
                start[rows, :] = jnp.broadcast_to(base, (8, SLOTS))

    def flag(over):
        bad[0:8, :] = jnp.maximum(bad[0:8, :], jnp.broadcast_to(jnp.where(over, 1.0, 0.0), (8, SLOTS)))

    def lists_far():
        def copy_row(r, c):
            for n, f in enumerate((0, 1, 2, 3, 6)):
                natural[n, r, pl.ds(c, 1), :] = field[0][r, c, f : f + 1, :]

        def step(c, carry):
            copy_row(0, c)
            copy_row(ROWS + 1, c)
            return carry

        lax.fori_loop(0, COLS + 2, step, 0)
        for r in range(1, ROWS + 1):
            copy_row(r, 0)
            copy_row(r, COLS + 1)
        first = ROWS * NEAR * COLS
        row = lax.broadcasted_iota(jnp.int32, (COLS, 1), 0)
        masks = []
        for a in range(ROWS):
            low, high = extents(a)
            masks += [near(beside(a, k, every), low, high) for k in range(NEAR, 8)]
            masks += [jnp.where(row == b, near(beside(a, k, every), low, high), 0.0) for k, b in PAST]
        count_up(masks, first)
        width = 8 - NEAR + len(PAST)
        for a in range(ROWS):
            for g in range(COLS // 8):
                rows = slice(a * COLS + 8 * g, a * COLS + 8 * g + 8)
                base = start[rows, 0:1]
                for n in range(width):
                    past = n >= 8 - NEAR
                    k, b = PAST[n - 8 + NEAR] if past else (NEAR + n, None)
                    if past and b // 8 != g:
                        continue
                    at = first + (a * width + n) * COLS + 8 * g
                    table = ranks[at : at + 8, :]
                    for t in range(TILES):
                        found = find(table, base, t)
                        if past:
                            found = jnp.where(found >= 0, found, code[t, k, rows, :])
                        code[t, k, rows, :] = found
                    base = base + table[:, SLOTS - 1 : SLOTS]
                flag(base > TILES * SLOTS)

    field_row = lax.broadcasted_iota(jnp.int32, (FIELDS, SLOTS), 0)

    def place(v):
        if isinstance(v, int):
            if v < ROWS * INNER:
                return v // INNER, v % INNER + 1
            return (v - ROWS * INNER) // 2, (v - ROWS * INNER) % 2 * (COLS - 1)
        a = jnp.where(v >= INNER, 1, 0)
        e = v - ROWS * INNER
        last = e >= 0
        a = jnp.where(last, lax.shift_right_logical(jnp.maximum(e, 0), 1), a)
        return a, jnp.where(last, lax.bitwise_and(e, 1) * (COLS - 1), v - INNER * a + 1)

    def broadcast_own(s, c, dst):
        a, b = place(c)
        mine = own_p[2 * a + (b // 8 if isinstance(b, int) else lax.shift_right_logical(b, 3))]
        at = lax.broadcasted_iota(jnp.int32, mine.shape, 1) & 7
        mine = jnp.where(at == (b & 7), mine.astype(f32), 0.0).astype(jnp.bfloat16)
        wide = jnp.dot(mine, pick[...], preferred_element_type=f32)
        for f in range(OWN_FIELDS):
            dst[f] = wide[:, f * SLOTS : (f + 1) * SLOTS]

    def sweep(own_at, start_at, tiles, finish):
        for i0 in range(0, SLOTS, BLOCK):
            here = pl.ds(i0, BLOCK)
            own = own_at(here)
            totals = start_at(here)
            for rows in tiles:
                totals = pair_terms(own, rows, totals)
            finish(here, totals)

    def rows_of(tile):
        return [tile[f : f + 1, :] for f in range(6)]

    def from_zero(here):
        return zeros, zeros, zeros

    def own_of(bc):
        return lambda here: [bc[f, here, :] for f in range(OWN_FIELDS)]

    def to_acc(acc):
        def finish(here, totals):
            for f in range(3):
                acc[f, here, :] = totals[f]

        return finish

    along_y = [jnp.where(field_row == 1, db * unit, 0.0) for _, db in LISTED]

    def pack(s, c, t, sides_of, packed, inside):
        a, b = place(c)
        inward = 1 - 2 * a
        x_shift = jnp.where(field_row == 0, unit * (inward * 1.0), 0.0)
        for k in sides_of:
            way, db = LISTED[k]
            at_b = b + 1 + db
            if inside:
                at_b = jnp.clip(at_b, 1, COLS)
            take = jnp.broadcast_to(code[t, k, pl.ds(a * COLS + b, 1), :], (FIELDS, SLOTS))
            moved = lane_gather(field[s][a + 1 + way * inward, at_b], take & (SLOTS - 1))
            if way > 0:
                moved = moved + x_shift
            elif way < 0:
                moved = moved - x_shift
            if db:
                moved = moved + along_y[k]
            packed = jnp.where(take >= 0, moved, packed)
        return packed

    nothing = jnp.zeros((FIELDS, SLOTS), f32)

    def early(s):
        broadcast_own(s, 0, bcs[0].at[0])

        def some(u, carry):
            for n in range(WAYS):
                c = WAYS * u + n
                a, b = place(c)
                broadcast_own(s, jnp.minimum(c + 1, CELLS - 1), bcs[(n + 1) % WAYS].at[u + (n + 1) // WAYS])
                rows = [field[s][a + 1, b + 1, f : f + 1, :] for f in range(6)]
                sweep(own_of(bcs[n].at[u]), from_zero, [rows], to_acc(accs[n].at[u]))
            return carry

        lax.fori_loop(0, TURNS, some, 0)

    def collect(c, acc, valid):
        a, b = place(c)
        if valid is not True:
            b = jnp.where(valid, b, -4 * SLOTS)
        for i0 in range(0, SLOTS, BLOCK):
            here = pl.ds(i0, BLOCK)
            rates = rate_t[a, here, :]
            for f in range(3):
                rates = jnp.where(lanes == f * COLS + b, jnp.sum(acc[f, here, :], 1, keepdims=True), rates)
            rate_t[a, here, :] = rates

    def late(s, relay, rest_of_halo):
        def pack_all(c, dst):
            for t in range(TILES):
                dst[t] = pack(s, c, t, range(8), nothing, False)

        def begin(u):
            for n in range(WAYS):
                pack_all(WAYS * u + n, lates[n].at[u])

        def some(last, u, carry):
            for n in range(WAYS):
                c = WAYS * u + n
                if n == 0:
                    w = jnp.maximum(u - 1, 0)
                    collect(jnp.maximum(c - 1, 0), accs[WAYS - 1].at[w], u > 0)
                else:
                    collect(c - 1, accs[n - 1].at[u], True)
                tiles = [rows_of(lates[n].at[u, t]) for t in range(TILES)]
                acc = accs[n].at[u]

                def start_at(here):
                    return tuple(acc[f, here, :] for f in range(3))

                sweep(own_of(bcs[n].at[u]), start_at, tiles, to_acc(acc))
                pack_all(jnp.minimum(c + WAYS, last - WAYS + n), lates[n].at[u + 1])
            return carry

        begin(0)
        lax.fori_loop(0, 2, functools.partial(some, ROWS * INNER), 0)
        relay()
        lax.fori_loop(2, INNER_TURNS, functools.partial(some, ROWS * INNER), 0)
        rest_of_halo()
        begin(INNER_TURNS)
        lax.fori_loop(INNER_TURNS, TURNS, functools.partial(some, CELLS), 0)
        collect(CELLS - 1, accs[WAYS - 1].at[TURNS - 1], True)

    def update(s, step):
        for a in range(ROWS):
            rates = rate_t[a].T
            occ = occ_ref[a]
            keep = keep_ref[a]
            rho = o_den[a]
            gain = step * occ
            scale = vel_coef / (rho + 1.0 - occ)
            o_den[a] = rho + gain * (rho_coef * rho * rates[0:COLS])
            vx = (o_vel[0, a] + gain * (scale * rates[COLS : 2 * COLS])) * keep
            vy = (o_vel[1, a] + gain * (scale * rates[2 * COLS : 3 * COLS] - gravity_accel)) * keep
            o_vel[0, a] = vx
            o_vel[1, a] = vy
            o_off[0, a] = o_off[0, a] + gain * vx
            o_off[1, a] = o_off[1, a] + gain * vy

    me_a = gx * 2 + core
    me_b = plane
    for s in range(ITERS):
        fastest(s)
        copies = halo(s)
        if s == 0:
            publish(s)
            if ring:
                boxes()
                lists_near()
                turn()
            pl.semaphore_wait(barrier, len(peers_a) + len(peers_b) + len(sides))
            spread(s, peers_a, msg_a, slot_a, me_a, a_send, a_recv)
        else:
            spread(s, peers_a, msg_a, slot_a, me_a, a_send, a_recv)
            publish(s)
        for copy in copies:
            copy.start()
        if ring:
            if s > 0:
                turn()
            early(s)

        def relay():
            gathered(s, peers_a, slot_a, a_send, a_recv).wait_recv()
            msg_b[s] = jnp.max(slot_a[s], axis=0)
            spread(s, peers_b, msg_b, slot_b, me_b, b_send, b_recv)

        if s == 0 or not ring:
            relay()
        for copy, (a, b) in zip(copies, SIDES):
            if b == 0:
                copy.wait_recv()
        clear_rows(s)

        def rest_of_halo():
            for copy, (a, b) in zip(copies, SIDES):
                if b != 0:
                    copy.wait_recv()
            clear_columns(s)

        if not ring:
            rest_of_halo()
            dense(s)
        elif s == 0:
            rest_of_halo()
            lists_far()
            late(s, lambda: None, lambda: None)
        else:
            late(s, relay, rest_of_halo)
        gathered(s, peers_b, slot_b, b_send, b_recv).wait_recv()
        result = jnp.max(slot_b[s], axis=0)
        top = 10.0 + jnp.sqrt(result[:, 0:1])
        update(s, courant * smoothing / top)
        if ring and s < ITERS - 1:
            check()
        for copy in copies:
            copy.wait_send()
        gathered(s, peers_a, slot_a, a_send, a_recv).wait_send()
        gathered(s, peers_b, slot_b, b_send, b_recv).wait_send()
    o_flag[...] = result


def substeps(ring, n_gx, n_gy, offsets, density, velocity, counts, walls):
    shape = jax.ShapeDtypeStruct
    dma = pltpu.SemaphoreType.DMA
    f32 = jnp.float32
    n_a, n_b = 2 * n_gx, n_gy // 2
    if ring:
        extra = [
            pltpu.VMEM((2 * ROWS, SLOTS, SLOTS), jnp.bfloat16),
            pltpu.VMEM((SLOTS, OWN_FIELDS * SLOTS), jnp.bfloat16),
            pltpu.VMEM((TILES, 8, CELLS, SLOTS), jnp.int32),
            pltpu.VMEM((5, ROWS + 2, 24, SLOTS), f32),
            pltpu.VMEM((ROWS * (8 + len(PAST)) * COLS, SLOTS), jnp.int32),
            pltpu.VMEM((CELLS, SLOTS), jnp.int32),
            pltpu.VMEM((2, ROWS, COLS, SLOTS), f32),
            pltpu.VMEM((2, ROWS, COLS, SLOTS), f32),
            pltpu.VMEM((COLS, SLOTS), f32),
        ]
        for per_cell in ((OWN_FIELDS, SLOTS, SLOTS), (3, SLOTS, SLOTS), (TILES, FIELDS, SLOTS)):
            extra += [pltpu.VMEM((TURNS + 1,) + per_cell, f32)] * WAYS
    else:
        extra = [pltpu.VMEM((ROWS, SLOTS, SLOTS), f32)]
    return pl.pallas_call(
        functools.partial(kernel, ring),
        out_shape=(
            shape(offsets.shape, f32),
            shape(density.shape, f32),
            shape(velocity.shape, f32),
            shape((1, SLOTS), f32),
        ),
        in_specs=[pl.BlockSpec(memory_space=pltpu.VMEM)] * 5,
        out_specs=tuple(pl.BlockSpec(memory_space=pltpu.VMEM) for _ in range(4)),
        scratch_shapes=[
            pltpu.VMEM((ROWS + 2, COLS + 2, FIELDS, SLOTS), f32),
            pltpu.VMEM((ROWS + 2, COLS + 2, FIELDS, SLOTS), f32),
            pltpu.VMEM((ROWS + 2, COLS + 2, FIELDS, SLOTS), f32),
            pltpu.VMEM((ROWS, SLOTS, SLOTS), f32),
            pltpu.VMEM((ROWS, COLS, SLOTS), f32),
            pltpu.VMEM((ROWS, COLS, SLOTS), f32),
            pltpu.VMEM((ITERS, 1, SLOTS), f32),
            pltpu.VMEM((ITERS, 1, SLOTS), f32),
            pltpu.VMEM((ITERS, n_a, 1, SLOTS), f32),
            pltpu.VMEM((ITERS, n_b, 1, SLOTS), f32),
            dma((ITERS, 8)),
            dma((ITERS, 8)),
            dma((ITERS,)),
            dma((ITERS,)),
            dma((ITERS,)),
            dma((ITERS,)),
        ]
        + extra,
        compiler_params=pltpu.CompilerParams(collective_id=0 if ring else 1, has_side_effects=True),
    )(offsets, density, velocity, counts, walls)


def shards(n_gx, n_gy, *args):
    *fast, flag = substeps(True, n_gx, n_gy, *args)
    return lax.cond(
        flag[0, SLOTS - 1] > 0.0,
        lambda: tuple(substeps(False, n_gx, n_gy, *args)[:3]),
        lambda: tuple(fast),
    )


def solution(mesh):
    fields = P(None, "gx", "gy", None)
    cells = P("gx", "gy")
    return jax.shard_map(
        functools.partial(shards, mesh.shape["gx"], mesh.shape["gy"]),
        mesh=mesh,
        in_specs=(fields, P("gx", "gy", None), fields, cells, cells),
        out_specs=(fields, P("gx", "gy", None), fields),
        check_vma=False,
    )
```

```python
import functools
import math

import jax
import jax.numpy as jnp
from jax import lax
from jax.experimental import pallas as pl
from jax.experimental.pallas import tpu as pltpu
from jax.sharding import PartitionSpec as P

ITERS = 3
ROWS = 2
COLS = 16
SLOTS = 128
FIELDS = 8
BLOCK = 16
OWN_FIELDS = 5
CELLS = ROWS * COLS
WAYS = 2
TURNS = CELLS // WAYS
INNER = COLS - 2
INNER_TURNS = ROWS * INNER // WAYS
TILES = 2
LISTED = ((0, -1), (0, 1), (1, -1), (1, 0), (1, 1), (-1, -1), (-1, 0), (-1, 1))
NEAR = 5
PAST = tuple((k, 0 if LISTED[k][1] < 0 else COLS - 1) for k in range(NEAR) if LISTED[k][1] != 0)
MESH = pl.DeviceIdType.MESH

courant = 0.2
smoothing = 0.1625
gravity_accel = 9.81
kernel_norm = 7.0 / (4.0 * math.pi * smoothing * smoothing)
grad_coef = -5.0 * kernel_norm / (smoothing * smoothing)
unit = 1.0 / (2.0 * smoothing)
rho_coef = 2.0 * grad_coef * smoothing
vel_coef = -2.0 * grad_coef * 2.0 * smoothing * 5.0
longest = 2.0 * courant * smoothing / 10.0
margin = 0.01
SIDES = tuple((a, b) for a in (-1, 0, 1) for b in (-1, 0, 1) if (a, b) != (0, 0))


def column(row):
    wide = jnp.broadcast_to(row, (COLS, COLS))
    r = lax.broadcasted_iota(jnp.int32, (COLS, COLS), 0)
    c = lax.broadcasted_iota(jnp.int32, (COLS, COLS), 1)
    return jnp.sum(jnp.where(r == c, wide, 0.0), axis=1, keepdims=True)


def pair_terms(own, other, totals):
    xi, yi, vxi, vyi, ppi = own
    xj, yj, vxj, vyj, ppj, wj = other
    ux = xi - xj
    uy = yi - yj
    u2 = ux * ux + uy * uy
    length = u2 * lax.rsqrt(jnp.maximum(u2, 1e-30))
    soft = lax.rsqrt(u2 + 0.0025)
    support = jnp.maximum(1.0 - length, 0.0)
    grad = (support * support) * (support * wj)
    along = (vxi - vxj) * ux + (vyi - vyj) * uy
    force = grad * ((ppi + ppj) - along * soft)
    return (
        totals[0] + grad * (along - (ppi - ppj) * length),
        totals[1] + force * ux,
        totals[2] + force * uy,
    )


def lane_gather(x, index):
    return lax.gather(
        x,
        index[..., None],
        lax.GatherDimensionNumbers(
            offset_dims=(),
            collapsed_slice_dims=(1,),
            start_index_map=(1,),
            operand_batching_dims=(0,),
            start_indices_batching_dims=(0,),
        ),
        slice_sizes=(1, 1),
        mode=lax.GatherScatterMode.PROMISE_IN_BOUNDS,
    )


def pieces(x):
    high = x.astype(jnp.bfloat16).astype(jnp.float32)
    rest = x - high
    middle = rest.astype(jnp.bfloat16).astype(jnp.float32)
    return high, middle, rest - middle


def kernel(
    ring, off, den, vel, cnt, wal, o_off, o_den, o_vel, o_flag,
    field0, field1, field2, rate_t, occ_ref, keep_ref, msg_a, msg_b, slot_a, slot_b,
    halo_send, halo_recv, a_send, a_recv, b_send, b_recv, *extra,
):
    f32 = jnp.float32
    field = (field0, field1, field2)
    if ring:
        own_p, pick, code, natural, ranks, start, box_lo, box_hi, bad, *ways = extra
        bcs, accs, lates = [ways[WAYS * n : WAYS * (n + 1)] for n in range(3)]
    else:
        (own_t,) = extra
    gx = lax.axis_index("gx")
    gy = lax.axis_index("gy")
    n_gx = lax.axis_size("gx")
    n_gy = lax.axis_size("gy")
    core = lax.rem(gy, 2)
    plane = lax.div(gy, 2)
    n_plane = n_gy // 2

    def side(a, b):
        return {"gx": lax.rem(gx + a + n_gx, n_gx), "gy": lax.rem(gy + b + n_gy, n_gy)}

    def peer_a(k):
        return {"gx": lax.rem(gx + k // 2, n_gx), "gy": plane * 2 + (lax.rem(core + 1, 2) if k % 2 else core)}

    def peer_b(k):
        return {"gx": gx, "gy": lax.rem(plane + k, n_plane) * 2 + core}

    peers_a = [peer_a(k) for k in range(1, 2 * n_gx)]
    peers_b = [peer_b(k) for k in range(1, n_plane)]
    sides = [side(a, b) for a, b in SIDES]

    barrier = pltpu.get_barrier_semaphore()
    for target in peers_a + peers_b + sides:
        pl.semaphore_signal(barrier, inc=1, device_id=target, device_id_type=MESH)

    lane = lax.broadcasted_iota(jnp.int32, (COLS, SLOTS), 1)
    lane_row = lax.broadcasted_iota(jnp.int32, (1, SLOTS), 1)
    for a in range(ROWS):
        occ = (lane.astype(f32) < column(cnt[a : a + 1, :].astype(f32))).astype(f32)
        keep = jnp.broadcast_to(column(1.0 - wal[a : a + 1, :].astype(f32)), (COLS, SLOTS))
        occ_ref[a] = occ
        keep_ref[a] = keep
        for c in range(2):
            o_off[c, a] = off[c, a]
            o_vel[c, a] = vel[c, a] * keep
        o_den[a] = den[a]
    rate_t[...] = jnp.zeros_like(rate_t)
    for later in field[1:]:
        later[1 : ROWS + 1, 1 : COLS + 1] = jnp.zeros((ROWS, COLS, FIELDS, SLOTS), f32)
    if ring:
        bad[...] = jnp.zeros_like(bad)
        natural[...] = jnp.zeros_like(natural)
        r = lax.broadcasted_iota(jnp.int32, pick.shape, 0)
        c = lax.broadcasted_iota(jnp.int32, pick.shape, 1)
        group = r // 8
        hit = (group % OWN_FIELDS == c // SLOTS) & (group < 3 * OWN_FIELDS)
        pick[...] = jnp.where(hit, 1.0, 0.0).astype(jnp.bfloat16)

    def fastest(s):
        best = jnp.zeros((COLS, SLOTS), f32)
        for a in range(ROWS):
            vx = o_vel[0, a]
            vy = o_vel[1, a]
            best = jnp.maximum(best, occ_ref[a] * (vx * vx + vy * vy))
        best = jnp.max(best, keepdims=True).reshape(1, 1)
        if ring:
            msg_a[s] = jnp.where(lane_row < SLOTS // 2, best, jnp.max(bad[...], keepdims=True).reshape(1, 1))
        else:
            msg_a[s] = jnp.broadcast_to(best, (1, SLOTS))

    def publish(s):
        for a in range(ROWS):
            occ = occ_ref[a]
            rho = o_den[a]
            rows = [
                o_off[0, a] * unit,
                o_off[1, a] * unit,
                o_vel[0, a],
                o_vel[1, a],
                10.0 * (rho - 1.0),
                occ / (64.0 * (rho + 1.0 - occ)),
                occ,
                jnp.zeros_like(occ),
            ]
            for f in range(FIELDS if s == 0 else 6):
                for b in range(COLS):
                    field[s][a + 1, b + 1, f : f + 1, :] = rows[f][b : b + 1]
            if not ring:
                own_t[a] = jnp.concatenate(rows, 0).T

    def turn():
        for a in range(ROWS):
            rows = [o_off[0, a] * unit, o_off[1, a] * unit, o_vel[0, a], o_vel[1, a], 10.0 * (o_den[a] - 1.0)]
            parts = [pieces(x) for x in rows]
            for h in range(2):
                flat = [p[n][8 * h : 8 * h + 8] for n in range(3) for p in parts]
                flat.append(jnp.zeros((8, SLOTS), f32))
                own_p[2 * a + h] = jnp.concatenate(flat, 0).T.astype(jnp.bfloat16)

    def halo(s):
        copies = []
        for k, (a, b) in enumerate(SIDES):
            src_r = pl.ds(1, 2) if a == 0 else (1 if a < 0 else 2)
            dst_r = pl.ds(1, 2) if a == 0 else (3 if a < 0 else 0)
            src_c = pl.ds(1, COLS) if b == 0 else (1 if b < 0 else COLS)
            dst_c = pl.ds(1, COLS) if b == 0 else (COLS + 1 if b < 0 else 0)
            sent = slice(0, FIELDS if s == 0 else 6)
            copies.append(
                pltpu.make_async_remote_copy(
                    src_ref=field[s].at[src_r, src_c, sent],
                    dst_ref=field[s].at[dst_r, dst_c, sent],
                    send_sem=halo_send.at[s, k],
                    recv_sem=halo_recv.at[s, k],
                    device_id=sides[k],
                    device_id_type=MESH,
                )
            )
        return copies

    def spread(s, peers, msg, slots, me, send, recv):
        slots[s, me] = msg[s]
        for target in peers:
            pltpu.make_async_remote_copy(
                src_ref=msg.at[s], dst_ref=slots.at[s, me], send_sem=send.at[s], recv_sem=recv.at[s],
                device_id=target, device_id_type=MESH,
            ).start()

    def gathered(s, peers, slots, send, recv):
        n = len(peers)
        whole = slots.at[s, pl.ds(0, n)]
        return pltpu.make_async_remote_copy(
            src_ref=whole, dst_ref=whole, send_sem=send.at[s], recv_sem=recv.at[s],
            device_id=peers[0], device_id_type=MESH,
        )

    def clear_rows(s):
        empty = jnp.zeros((COLS, FIELDS, SLOTS), f32)

        @pl.when(gx == 0)
        def _():
            field[s][0, 1 : COLS + 1] = empty

        @pl.when(gx == n_gx - 1)
        def _():
            field[s][ROWS + 1, 1 : COLS + 1] = empty

    def clear_columns(s):
        empty = jnp.zeros((FIELDS, SLOTS), f32)
        for at, end in ((0, 0), (ROWS + 1, n_gx - 1)):

            @pl.when(gx == end)
            def _():
                field[s][at, 0] = empty
                field[s][at, COLS + 1] = empty

        for at, end in ((0, 0), (COLS + 1, n_gy - 1)):

            @pl.when(gy == end)
            def _():
                for r in range(ROWS + 2):
                    field[s][r, at] = empty

    lanes = lax.broadcasted_iota(jnp.int32, (BLOCK, SLOTS), 1)
    zeros = jnp.zeros((BLOCK, SLOTS), f32)

    def dense(s):
        def tile(t, carry):
            a = lax.div(t, SLOTS // BLOCK)
            i0 = pl.multiple_of(lax.rem(t, SLOTS // BLOCK) * BLOCK, BLOCK)
            mine = own_t[a, pl.ds(i0, BLOCK), :]

            def cell(b, rates):
                turned = pltpu.roll(mine, lax.rem(SLOTS - b, SLOTS), 1)
                own = [jnp.broadcast_to(turned[:, COLS * f : COLS * f + 1], (BLOCK, SLOTS)) for f in range(5)]
                totals = (zeros, zeros, zeros)
                for da in range(3):
                    for db in range(3):
                        rows = [field[s][a + da, b + db, f : f + 1, :] for f in range(6)]
                        rows[0] = rows[0] + (da - 1) * unit
                        rows[1] = rows[1] + (db - 1) * unit
                        totals = pair_terms(own, rows, totals)
                for f in range(3):
                    rates = jnp.where(lanes == f * COLS + b, jnp.sum(totals[f], 1, keepdims=True), rates)
                return rates

            rate_t[a, pl.ds(i0, BLOCK), :] = lax.fori_loop(0, COLS, cell, zeros)
            return carry

        lax.fori_loop(0, ROWS * SLOTS // BLOCK, tile, 0)

    def boxes():
        for a in range(ROWS):
            for d in range(2):
                x = o_off[d, a] * unit
                way = o_vel[d, a] * (longest * unit)
                box_lo[d, a] = x + jnp.minimum(way, 0.0) - margin * unit
                box_hi[d, a] = x + jnp.maximum(way, 0.0) + margin * unit

    def check():
        for a in range(ROWS):
            inside = occ_ref[a] < 0.5
            both = None
            for d in range(2):
                x = o_off[d, a] * unit
                within = (x >= box_lo[d, a]) & (x <= box_hi[d, a])
                both = within if both is None else both & within
            bad[...] = jnp.maximum(bad[...], jnp.where(inside | both, 0.0, 1.0))

    def near(there, low, high):
        hit = there[4] > 0.5
        for d in range(2):
            way = there[2 + d] * (longest * unit)
            hit = hit & (there[d] + jnp.maximum(way, 0.0) + margin * unit > low[d])
            hit = hit & (there[d] + jnp.minimum(way, 0.0) - margin * unit < high[d])
        return jnp.where(hit, 1.0, 0.0)

    def extents(a):
        occ = occ_ref[a] > 0.5
        reach = 1.0001
        low = [jnp.min(jnp.where(occ, box_lo[d, a], 1e30), axis=1, keepdims=True) - reach for d in range(2)]
        high = [jnp.max(jnp.where(occ, box_hi[d, a], -1e30), axis=1, keepdims=True) + reach for d in range(2)]
        return low, high

    def beside(a, k, rows):
        da = LISTED[k][0] * (1 - 2 * a)
        db = LISTED[k][1]
        there = [natural[n, a + 1 + da, 1 + db + rows.start : 1 + db + rows.stop, :] for n in range(5)]
        there[0] = there[0] + da * unit
        there[1] = there[1] + db * unit
        return there

    def count_up(masks, at):
        r = lax.broadcasted_iota(jnp.int32, (SLOTS, SLOTS), 0)
        c = lax.broadcasted_iota(jnp.int32, (SLOTS, SLOTS), 1)
        upper = jnp.where(r <= c, 1.0, 0.0).astype(jnp.bfloat16)
        stacked = jnp.concatenate(masks, 0).astype(jnp.bfloat16)
        ranks[at : at + stacked.shape[0], :] = jnp.dot(stacked, upper, preferred_element_type=f32).astype(jnp.int32)

    spread_lane = lax.broadcasted_iota(jnp.int32, (8, SLOTS), 1)

    def find(table, base, t):
        rank = spread_lane + (SLOTS * t + 1) - base
        spot = jnp.zeros((8, SLOTS), jnp.int32)
        for bit in (64, 32, 16, 8, 4, 2, 1):
            probe = lane_gather(table, spot + (bit - 1))
            spot = jnp.where(probe < rank, spot + bit, spot)
        return jnp.where((rank >= 1) & (rank <= table[:, SLOTS - 1 : SLOTS]), spot, -1)

    every = slice(0, COLS)

    def lists_near():
        for a in range(ROWS):
            whole = [o_off[0, a] * unit, o_off[1, a] * unit, o_vel[0, a], o_vel[1, a], occ_ref[a]]
            for n in range(5):
                natural[n, a + 1, 1 : COLS + 1, :] = whole[n]
        masks = []
        for a in range(ROWS):
            low, high = extents(a)
            masks += [near(beside(a, k, every), low, high) for k in range(NEAR)]
        count_up(masks, 0)
        for a in range(ROWS):
            for g in range(COLS // 8):
                rows = slice(a * COLS + 8 * g, a * COLS + 8 * g + 8)
                base = jnp.zeros((8, 1), jnp.int32)
                for k in range(NEAR):
                    at = (a * NEAR + k) * COLS + 8 * g
                    table = ranks[at : at + 8, :]
                    for t in range(TILES):
                        code[t, k, rows, :] = find(table, base, t)
                    base = base + table[:, SLOTS - 1 : SLOTS]
                start[rows, :] = jnp.broadcast_to(base, (8, SLOTS))

    def flag(over):
        bad[0:8, :] = jnp.maximum(bad[0:8, :], jnp.broadcast_to(jnp.where(over, 1.0, 0.0), (8, SLOTS)))

    def lists_far():
        def copy_row(r, c):
            for n, f in enumerate((0, 1, 2, 3, 6)):
                natural[n, r, pl.ds(c, 1), :] = field[0][r, c, f : f + 1, :]

        def step(c, carry):
            copy_row(0, c)
            copy_row(ROWS + 1, c)
            return carry

        lax.fori_loop(0, COLS + 2, step, 0)
        for r in range(1, ROWS + 1):
            copy_row(r, 0)
            copy_row(r, COLS + 1)
        first = ROWS * NEAR * COLS
        row = lax.broadcasted_iota(jnp.int32, (COLS, 1), 0)
        masks = []
        for a in range(ROWS):
            low, high = extents(a)
            masks += [near(beside(a, k, every), low, high) for k in range(NEAR, 8)]
            masks += [jnp.where(row == b, near(beside(a, k, every), low, high), 0.0) for k, b in PAST]
        count_up(masks, first)
        width = 8 - NEAR + len(PAST)
        for a in range(ROWS):
            for g in range(COLS // 8):
                rows = slice(a * COLS + 8 * g, a * COLS + 8 * g + 8)
                base = start[rows, 0:1]
                for n in range(width):
                    past = n >= 8 - NEAR
                    k, b = PAST[n - 8 + NEAR] if past else (NEAR + n, None)
                    if past and b // 8 != g:
                        continue
                    at = first + (a * width + n) * COLS + 8 * g
                    table = ranks[at : at + 8, :]
                    for t in range(TILES):
                        found = find(table, base, t)
                        if past:
                            found = jnp.where(found >= 0, found, code[t, k, rows, :])
                        code[t, k, rows, :] = found
                    base = base + table[:, SLOTS - 1 : SLOTS]
                flag(base > TILES * SLOTS)

    field_row = lax.broadcasted_iota(jnp.int32, (FIELDS, SLOTS), 0)

    def place(v):
        if isinstance(v, int):
            if v < ROWS * INNER:
                return v // INNER, v % INNER + 1
            return (v - ROWS * INNER) // 2, (v - ROWS * INNER) % 2 * (COLS - 1)
        a = jnp.where(v >= INNER, 1, 0)
        e = v - ROWS * INNER
        last = e >= 0
        a = jnp.where(last, lax.shift_right_logical(jnp.maximum(e, 0), 1), a)
        return a, jnp.where(last, lax.bitwise_and(e, 1) * (COLS - 1), v - INNER * a + 1)

    def broadcast_own(s, c, dst):
        a, b = place(c)
        mine = own_p[2 * a + (b // 8 if isinstance(b, int) else lax.shift_right_logical(b, 3))]
        at = lax.broadcasted_iota(jnp.int32, mine.shape, 1) & 7
        mine = jnp.where(at == (b & 7), mine.astype(f32), 0.0).astype(jnp.bfloat16)
        wide = jnp.dot(mine, pick[...], preferred_element_type=f32)
        for f in range(OWN_FIELDS):
            dst[f] = wide[:, f * SLOTS : (f + 1) * SLOTS]

    def sweep(own_at, start_at, tiles, finish):
        for i0 in range(0, SLOTS, BLOCK):
            here = pl.ds(i0, BLOCK)
            own = own_at(here)
            totals = start_at(here)
            for rows in tiles:
                totals = pair_terms(own, rows, totals)
            finish(here, totals)

    def rows_of(tile):
        return [tile[f : f + 1, :] for f in range(6)]

    def from_zero(here):
        return zeros, zeros, zeros

    def own_of(bc):
        return lambda here: [bc[f, here, :] for f in range(OWN_FIELDS)]

    def to_acc(acc):
        def finish(here, totals):
            for f in range(3):
                acc[f, here, :] = totals[f]

        return finish

    along_y = [jnp.where(field_row == 1, db * unit, 0.0) for _, db in LISTED]

    def pack(s, c, t, sides_of, packed, inside):
        a, b = place(c)
        inward = 1 - 2 * a
        x_shift = jnp.where(field_row == 0, unit * (inward * 1.0), 0.0)
        for k in sides_of:
            way, db = LISTED[k]
            at_b = b + 1 + db
            if inside:
                at_b = jnp.clip(at_b, 1, COLS)
            take = jnp.broadcast_to(code[t, k, pl.ds(a * COLS + b, 1), :], (FIELDS, SLOTS))
            moved = lane_gather(field[s][a + 1 + way * inward, at_b], take & (SLOTS - 1))
            if way > 0:
                moved = moved + x_shift
            elif way < 0:
                moved = moved - x_shift
            if db:
                moved = moved + along_y[k]
            packed = jnp.where(take >= 0, moved, packed)
        return packed

    nothing = jnp.zeros((FIELDS, SLOTS), f32)

    def early(s):
        broadcast_own(s, 0, bcs[0].at[0])

        def some(u, carry):
            for n in range(WAYS):
                c = WAYS * u + n
                a, b = place(c)
                broadcast_own(s, jnp.minimum(c + 1, CELLS - 1), bcs[(n + 1) % WAYS].at[u + (n + 1) // WAYS])
                rows = [field[s][a + 1, b + 1, f : f + 1, :] for f in range(6)]
                sweep(own_of(bcs[n].at[u]), from_zero, [rows], to_acc(accs[n].at[u]))
            return carry

        lax.fori_loop(0, TURNS, some, 0)

    def collect(c, acc, valid):
        a, b = place(c)
        if valid is not True:
            b = jnp.where(valid, b, -4 * SLOTS)
        for i0 in range(0, SLOTS, BLOCK):
            here = pl.ds(i0, BLOCK)
            rates = rate_t[a, here, :]
            for f in range(3):
                rates = jnp.where(lanes == f * COLS + b, jnp.sum(acc[f, here, :], 1, keepdims=True), rates)
            rate_t[a, here, :] = rates

    def late(s, relay, rest_of_halo):
        def pack_all(c, dst):
            for t in range(TILES):
                dst[t] = pack(s, c, t, range(8), nothing, False)

        def begin(u):
            for n in range(WAYS):
                pack_all(WAYS * u + n, lates[n].at[u])

        def some(last, u, carry):
            for n in range(WAYS):
                c = WAYS * u + n
                if n == 0:
                    w = jnp.maximum(u - 1, 0)
                    collect(jnp.maximum(c - 1, 0), accs[WAYS - 1].at[w], u > 0)
                else:
                    collect(c - 1, accs[n - 1].at[u], True)
                tiles = [rows_of(lates[n].at[u, t]) for t in range(TILES)]
                acc = accs[n].at[u]

                def start_at(here):
                    return tuple(acc[f, here, :] for f in range(3))

                sweep(own_of(bcs[n].at[u]), start_at, tiles, to_acc(acc))
                pack_all(jnp.minimum(c + WAYS, last - WAYS + n), lates[n].at[u + 1])
            return carry

        begin(0)
        lax.fori_loop(0, 2, functools.partial(some, ROWS * INNER), 0)
        relay()
        lax.fori_loop(2, INNER_TURNS, functools.partial(some, ROWS * INNER), 0)
        rest_of_halo()
        begin(INNER_TURNS)
        lax.fori_loop(INNER_TURNS, TURNS, functools.partial(some, CELLS), 0)
        collect(CELLS - 1, accs[WAYS - 1].at[TURNS - 1], True)

    def update(s, step):
        for a in range(ROWS):
            rates = rate_t[a].T
            occ = occ_ref[a]
            keep = keep_ref[a]
            rho = o_den[a]
            gain = step * occ
            scale = vel_coef / (rho + 1.0 - occ)
            o_den[a] = rho + gain * (rho_coef * rho * rates[0:COLS])
            vx = (o_vel[0, a] + gain * (scale * rates[COLS : 2 * COLS])) * keep
            vy = (o_vel[1, a] + gain * (scale * rates[2 * COLS : 3 * COLS] - gravity_accel)) * keep
            o_vel[0, a] = vx
            o_vel[1, a] = vy
            o_off[0, a] = o_off[0, a] + gain * vx
            o_off[1, a] = o_off[1, a] + gain * vy

    me_a = gx * 2 + core
    me_b = plane
    for s in range(ITERS):
        fastest(s)
        copies = halo(s)
        if s == 0:
            publish(s)
            if ring:
                boxes()
                lists_near()
                turn()
            pl.semaphore_wait(barrier, len(peers_a) + len(peers_b) + len(sides))
            spread(s, peers_a, msg_a, slot_a, me_a, a_send, a_recv)
        else:
            spread(s, peers_a, msg_a, slot_a, me_a, a_send, a_recv)
            publish(s)
        for copy in copies:
            copy.start()
        if ring:
            if s > 0:
                turn()
            early(s)

        def relay():
            gathered(s, peers_a, slot_a, a_send, a_recv).wait_recv()
            msg_b[s] = jnp.max(slot_a[s], axis=0)
            spread(s, peers_b, msg_b, slot_b, me_b, b_send, b_recv)

        if s == 0 or not ring:
            relay()
        for copy, (a, b) in zip(copies, SIDES):
            if b == 0:
                copy.wait_recv()
        clear_rows(s)

        def rest_of_halo():
            for copy, (a, b) in zip(copies, SIDES):
                if b != 0:
                    copy.wait_recv()
            clear_columns(s)

        if not ring:
            rest_of_halo()
            dense(s)
        elif s == 0:
            rest_of_halo()
            lists_far()
            late(s, lambda: None, lambda: None)
        else:
            late(s, relay, rest_of_halo)
        gathered(s, peers_b, slot_b, b_send, b_recv).wait_recv()
        result = jnp.max(slot_b[s], axis=0)
        top = 10.0 + jnp.sqrt(result[:, 0:1])
        update(s, courant * smoothing / top)
        if ring and s < ITERS - 1:
            check()
        for copy in copies:
            copy.wait_send()
        gathered(s, peers_a, slot_a, a_send, a_recv).wait_send()
        gathered(s, peers_b, slot_b, b_send, b_recv).wait_send()
    o_flag[0, 0] = jnp.max(result[:, SLOTS // 2 :])


def substeps(ring, n_gx, n_gy, offsets, density, velocity, counts, walls):
    shape = jax.ShapeDtypeStruct
    dma = pltpu.SemaphoreType.DMA
    f32 = jnp.float32
    n_a, n_b = 2 * n_gx, n_gy // 2
    if ring:
        extra = [
            pltpu.VMEM((2 * ROWS, SLOTS, SLOTS), jnp.bfloat16),
            pltpu.VMEM((SLOTS, OWN_FIELDS * SLOTS), jnp.bfloat16),
            pltpu.VMEM((TILES, 8, CELLS, SLOTS), jnp.int32),
            pltpu.VMEM((5, ROWS + 2, 24, SLOTS), f32),
            pltpu.VMEM((ROWS * (8 + len(PAST)) * COLS, SLOTS), jnp.int32),
            pltpu.VMEM((CELLS, SLOTS), jnp.int32),
            pltpu.VMEM((2, ROWS, COLS, SLOTS), f32),
            pltpu.VMEM((2, ROWS, COLS, SLOTS), f32),
            pltpu.VMEM((COLS, SLOTS), f32),
        ]
        for per_cell in ((OWN_FIELDS, SLOTS, SLOTS), (3, SLOTS, SLOTS), (TILES, FIELDS, SLOTS)):
            extra += [pltpu.VMEM((TURNS + 1,) + per_cell, f32)] * WAYS
    else:
        extra = [pltpu.VMEM((ROWS, SLOTS, SLOTS), f32)]
    return pl.pallas_call(
        functools.partial(kernel, ring),
        out_shape=(
            shape(offsets.shape, f32),
            shape(density.shape, f32),
            shape(velocity.shape, f32),
            shape((1, 1), f32),
        ),
        in_specs=[pl.BlockSpec(memory_space=pltpu.VMEM)] * 5,
        out_specs=tuple(pl.BlockSpec(memory_space=pltpu.VMEM) for _ in range(3)) + (pl.BlockSpec(memory_space=pltpu.SMEM),),
        scratch_shapes=[
            pltpu.VMEM((ROWS + 2, COLS + 2, FIELDS, SLOTS), f32),
            pltpu.VMEM((ROWS + 2, COLS + 2, FIELDS, SLOTS), f32),
            pltpu.VMEM((ROWS + 2, COLS + 2, FIELDS, SLOTS), f32),
            pltpu.VMEM((ROWS, SLOTS, SLOTS), f32),
            pltpu.VMEM((ROWS, COLS, SLOTS), f32),
            pltpu.VMEM((ROWS, COLS, SLOTS), f32),
            pltpu.VMEM((ITERS, 1, SLOTS), f32),
            pltpu.VMEM((ITERS, 1, SLOTS), f32),
            pltpu.VMEM((ITERS, n_a, 1, SLOTS), f32),
            pltpu.VMEM((ITERS, n_b, 1, SLOTS), f32),
            dma((ITERS, 8)),
            dma((ITERS, 8)),
            dma((ITERS,)),
            dma((ITERS,)),
            dma((ITERS,)),
            dma((ITERS,)),
        ]
        + extra,
        compiler_params=pltpu.CompilerParams(collective_id=0 if ring else 1, has_side_effects=True),
    )(offsets, density, velocity, counts, walls)


def shards(n_gx, n_gy, *args):
    *fast, flag = substeps(True, n_gx, n_gy, *args)
    return lax.cond(
        flag[0, 0] > 0.0,
        lambda: tuple(substeps(False, n_gx, n_gy, *args)[:3]),
        lambda: tuple(fast),
    )


def solution(mesh):
    fields = P(None, "gx", "gy", None)
    cells = P("gx", "gy")
    return jax.shard_map(
        functools.partial(shards, mesh.shape["gx"], mesh.shape["gy"]),
        mesh=mesh,
        in_specs=(fields, P("gx", "gy", None), fields, cells, cells),
        out_specs=(fields, P("gx", "gy", None), fields),
        check_vma=False,
    )
```

```python
import functools
import math

import jax
import jax.numpy as jnp
from jax import lax
from jax.experimental import pallas as pl
from jax.experimental.pallas import tpu as pltpu
from jax.sharding import PartitionSpec as P

ITERS = 3
ROWS = 2
COLS = 16
SLOTS = 128
FIELDS = 8
BLOCK = 16
OWN_FIELDS = 5
CELLS = ROWS * COLS
WAYS = 2
TURNS = CELLS // WAYS
INNER = COLS - 2
INNER_TURNS = ROWS * INNER // WAYS
TILES = 2
LISTED = ((0, -1), (0, 1), (1, -1), (1, 0), (1, 1), (-1, -1), (-1, 0), (-1, 1))
NEAR = 5
PAST = tuple((k, 0 if LISTED[k][1] < 0 else COLS - 1) for k in range(NEAR) if LISTED[k][1] != 0)
MESH = pl.DeviceIdType.MESH

courant = 0.2
smoothing = 0.1625
gravity_accel = 9.81
kernel_norm = 7.0 / (4.0 * math.pi * smoothing * smoothing)
grad_coef = -5.0 * kernel_norm / (smoothing * smoothing)
unit = 1.0 / (2.0 * smoothing)
rho_coef = 2.0 * grad_coef * smoothing
vel_coef = -2.0 * grad_coef * 2.0 * smoothing * 5.0
longest = 2.0 * courant * smoothing / 10.0
margin = 0.01
SIDES = tuple((a, b) for a in (-1, 0, 1) for b in (-1, 0, 1) if (a, b) != (0, 0))


def column(row):
    wide = jnp.broadcast_to(row, (COLS, COLS))
    r = lax.broadcasted_iota(jnp.int32, (COLS, COLS), 0)
    c = lax.broadcasted_iota(jnp.int32, (COLS, COLS), 1)
    return jnp.sum(jnp.where(r == c, wide, 0.0), axis=1, keepdims=True)


def pair_terms(own, other, totals):
    xi, yi, vxi, vyi, ppi = own
    xj, yj, vxj, vyj, ppj, wj = other
    ux = xi - xj
    uy = yi - yj
    u2 = ux * ux + uy * uy
    length = u2 * lax.rsqrt(jnp.maximum(u2, 1e-30))
    soft = lax.rsqrt(u2 + 0.0025)
    support = jnp.maximum(1.0 - length, 0.0)
    grad = (support * support) * (support * wj)
    along = (vxi - vxj) * ux + (vyi - vyj) * uy
    force = grad * ((ppi + ppj) - along * soft)
    return (
        totals[0] + grad * (along - (ppi - ppj) * length),
        totals[1] + force * ux,
        totals[2] + force * uy,
    )


def lane_gather(x, index):
    return lax.gather(
        x,
        index[..., None],
        lax.GatherDimensionNumbers(
            offset_dims=(),
            collapsed_slice_dims=(1,),
            start_index_map=(1,),
            operand_batching_dims=(0,),
            start_indices_batching_dims=(0,),
        ),
        slice_sizes=(1, 1),
        mode=lax.GatherScatterMode.PROMISE_IN_BOUNDS,
    )


def pieces(x):
    high = x.astype(jnp.bfloat16).astype(jnp.float32)
    rest = x - high
    middle = rest.astype(jnp.bfloat16).astype(jnp.float32)
    return high, middle, rest - middle


def kernel(
    ring, off, den, vel, cnt, wal, o_off, o_den, o_vel, o_flag,
    field0, field1, field2, rate_t, occ_ref, keep_ref, msg_a, msg_b, slot_a, slot_b,
    halo_send, halo_recv, a_send, a_recv, b_send, b_recv, *extra,
):
    f32 = jnp.float32
    field = (field0, field1, field2)
    if ring:
        own_p, pick, code, natural, ranks, start, box_lo, box_hi, bad, *ways = extra
        bcs, accs, lates = [ways[WAYS * n : WAYS * (n + 1)] for n in range(3)]
    else:
        (own_t,) = extra
    gx = lax.axis_index("gx")
    gy = lax.axis_index("gy")
    n_gx = lax.axis_size("gx")
    n_gy = lax.axis_size("gy")
    core = lax.rem(gy, 2)
    plane = lax.div(gy, 2)
    n_plane = n_gy // 2

    def side(a, b):
        return {"gx": lax.rem(gx + a + n_gx, n_gx), "gy": lax.rem(gy + b + n_gy, n_gy)}

    def peer_a(k):
        return {"gx": lax.rem(gx + k // 2, n_gx), "gy": plane * 2 + (lax.rem(core + 1, 2) if k % 2 else core)}

    def peer_b(k):
        return {"gx": gx, "gy": lax.rem(plane + k, n_plane) * 2 + core}

    peers_a = [peer_a(k) for k in range(1, 2 * n_gx)]
    peers_b = [peer_b(k) for k in range(1, n_plane)]
    sides = [side(a, b) for a, b in SIDES]

    barrier = pltpu.get_barrier_semaphore()
    for target in peers_a + peers_b + sides:
        pl.semaphore_signal(barrier, inc=1, device_id=target, device_id_type=MESH)

    lane = lax.broadcasted_iota(jnp.int32, (COLS, SLOTS), 1)
    lane_row = lax.broadcasted_iota(jnp.int32, (1, SLOTS), 1)
    for a in range(ROWS):
        occ = (lane.astype(f32) < column(cnt[a : a + 1, :].astype(f32))).astype(f32)
        keep = jnp.broadcast_to(column(1.0 - wal[a : a + 1, :].astype(f32)), (COLS, SLOTS))
        occ_ref[a] = occ
        keep_ref[a] = keep
        for c in range(2):
            o_off[c, a] = off[c, a]
            o_vel[c, a] = vel[c, a] * keep
        o_den[a] = den[a]
    rate_t[...] = jnp.zeros_like(rate_t)
    for later in field[1:]:
        later[1 : ROWS + 1, 1 : COLS + 1] = jnp.zeros((ROWS, COLS, FIELDS, SLOTS), f32)
    if ring:
        bad[...] = jnp.zeros_like(bad)
        natural[...] = jnp.zeros_like(natural)
        r = lax.broadcasted_iota(jnp.int32, pick.shape, 0)
        c = lax.broadcasted_iota(jnp.int32, pick.shape, 1)
        group = r // 8
        hit = (group % OWN_FIELDS == c // SLOTS) & (group < 3 * OWN_FIELDS)
        pick[...] = jnp.where(hit, 1.0, 0.0).astype(jnp.bfloat16)

    def fastest(s):
        best = jnp.zeros((COLS, SLOTS), f32)
        for a in range(ROWS):
            vx = o_vel[0, a]
            vy = o_vel[1, a]
            best = jnp.maximum(best, occ_ref[a] * (vx * vx + vy * vy))
        best = jnp.max(best, keepdims=True).reshape(1, 1)
        if ring:
            msg_a[s] = jnp.where(lane_row < SLOTS // 2, best, jnp.max(bad[...], keepdims=True).reshape(1, 1))
        else:
            msg_a[s] = jnp.broadcast_to(best, (1, SLOTS))

    def publish(s):
        for a in range(ROWS):
            occ = occ_ref[a]
            rho = o_den[a]
            rows = [
                o_off[0, a] * unit,
                o_off[1, a] * unit,
                o_vel[0, a],
                o_vel[1, a],
                10.0 * (rho - 1.0),
                occ / (64.0 * (rho + 1.0 - occ)),
                occ,
                jnp.zeros_like(occ),
            ]
            for f in range(FIELDS if s == 0 else 6):
                for b in range(COLS):
                    field[s][a + 1, b + 1, f : f + 1, :] = rows[f][b : b + 1]
            if not ring:
                own_t[a] = jnp.concatenate(rows, 0).T

    def turn():
        for a in range(ROWS):
            rows = [o_off[0, a] * unit, o_off[1, a] * unit, o_vel[0, a], o_vel[1, a], 10.0 * (o_den[a] - 1.0)]
            parts = [pieces(x) for x in rows]
            for h in range(2):
                flat = [p[n][8 * h : 8 * h + 8] for n in range(3) for p in parts]
                flat.append(jnp.zeros((8, SLOTS), f32))
                own_p[2 * a + h] = jnp.concatenate(flat, 0).T.astype(jnp.bfloat16)

    def halo(s):
        copies = []
        for k, (a, b) in enumerate(SIDES):
            src_r = pl.ds(1, 2) if a == 0 else (1 if a < 0 else 2)
            dst_r = pl.ds(1, 2) if a == 0 else (3 if a < 0 else 0)
            src_c = pl.ds(1, COLS) if b == 0 else (1 if b < 0 else COLS)
            dst_c = pl.ds(1, COLS) if b == 0 else (COLS + 1 if b < 0 else 0)
            sent = slice(0, FIELDS if s == 0 else 6)
            copies.append(
                pltpu.make_async_remote_copy(
                    src_ref=field[s].at[src_r, src_c, sent],
                    dst_ref=field[s].at[dst_r, dst_c, sent],
                    send_sem=halo_send.at[s, k],
                    recv_sem=halo_recv.at[s, k],
                    device_id=sides[k],
                    device_id_type=MESH,
                )
            )
        return copies

    def spread(s, peers, msg, slots, me, send, recv):
        slots[s, me] = msg[s]
        for target in peers:
            pltpu.make_async_remote_copy(
                src_ref=msg.at[s], dst_ref=slots.at[s, me], send_sem=send.at[s], recv_sem=recv.at[s],
                device_id=target, device_id_type=MESH,
            ).start()

    def gathered(s, peers, slots, send, recv):
        n = len(peers)
        whole = slots.at[s, pl.ds(0, n)]
        return pltpu.make_async_remote_copy(
            src_ref=whole, dst_ref=whole, send_sem=send.at[s], recv_sem=recv.at[s],
            device_id=peers[0], device_id_type=MESH,
        )

    def clear_rows(s):
        empty = jnp.zeros((COLS, FIELDS, SLOTS), f32)

        @pl.when(gx == 0)
        def _():
            field[s][0, 1 : COLS + 1] = empty

        @pl.when(gx == n_gx - 1)
        def _():
            field[s][ROWS + 1, 1 : COLS + 1] = empty

    def clear_columns(s):
        empty = jnp.zeros((FIELDS, SLOTS), f32)
        for at, end in ((0, 0), (ROWS + 1, n_gx - 1)):

            @pl.when(gx == end)
            def _():
                field[s][at, 0] = empty
                field[s][at, COLS + 1] = empty

        for at, end in ((0, 0), (COLS + 1, n_gy - 1)):

            @pl.when(gy == end)
            def _():
                for r in range(ROWS + 2):
                    field[s][r, at] = empty

    lanes = lax.broadcasted_iota(jnp.int32, (BLOCK, SLOTS), 1)
    zeros = jnp.zeros((BLOCK, SLOTS), f32)

    def dense(s):
        def tile(t, carry):
            a = lax.div(t, SLOTS // BLOCK)
            i0 = pl.multiple_of(lax.rem(t, SLOTS // BLOCK) * BLOCK, BLOCK)
            mine = own_t[a, pl.ds(i0, BLOCK), :]

            def cell(b, rates):
                turned = pltpu.roll(mine, lax.rem(SLOTS - b, SLOTS), 1)
                own = [jnp.broadcast_to(turned[:, COLS * f : COLS * f + 1], (BLOCK, SLOTS)) for f in range(5)]
                totals = (zeros, zeros, zeros)
                for da in range(3):
                    for db in range(3):
                        rows = [field[s][a + da, b + db, f : f + 1, :] for f in range(6)]
                        rows[0] = rows[0] + (da - 1) * unit
                        rows[1] = rows[1] + (db - 1) * unit
                        totals = pair_terms(own, rows, totals)
                for f in range(3):
                    rates = jnp.where(lanes == f * COLS + b, jnp.sum(totals[f], 1, keepdims=True), rates)
                return rates

            rate_t[a, pl.ds(i0, BLOCK), :] = lax.fori_loop(0, COLS, cell, zeros)
            return carry

        lax.fori_loop(0, ROWS * SLOTS // BLOCK, tile, 0)

    def boxes():
        for a in range(ROWS):
            for d in range(2):
                x = o_off[d, a] * unit
                way = o_vel[d, a] * (longest * unit)
                box_lo[d, a] = x + jnp.minimum(way, 0.0) - margin * unit
                box_hi[d, a] = x + jnp.maximum(way, 0.0) + margin * unit

    def check():
        for a in range(ROWS):
            inside = occ_ref[a] < 0.5
            both = None
            for d in range(2):
                x = o_off[d, a] * unit
                within = (x >= box_lo[d, a]) & (x <= box_hi[d, a])
                both = within if both is None else both & within
            bad[...] = jnp.maximum(bad[...], jnp.where(inside | both, 0.0, 1.0))

    def near(there, low, high):
        hit = there[4] > 0.5
        for d in range(2):
            way = there[2 + d] * (longest * unit)
            hit = hit & (there[d] + jnp.maximum(way, 0.0) + margin * unit > low[d])
            hit = hit & (there[d] + jnp.minimum(way, 0.0) - margin * unit < high[d])
        return jnp.where(hit, 1.0, 0.0)

    def extents(a):
        occ = occ_ref[a] > 0.5
        reach = 1.0001
        low = [jnp.min(jnp.where(occ, box_lo[d, a], 1e30), axis=1, keepdims=True) - reach for d in range(2)]
        high = [jnp.max(jnp.where(occ, box_hi[d, a], -1e30), axis=1, keepdims=True) + reach for d in range(2)]
        return low, high

    def beside(a, k, rows):
        da = LISTED[k][0] * (1 - 2 * a)
        db = LISTED[k][1]
        there = [natural[n, a + 1 + da, 1 + db + rows.start : 1 + db + rows.stop, :] for n in range(5)]
        there[0] = there[0] + da * unit
        there[1] = there[1] + db * unit
        return there

    def count_up(masks, at):
        r = lax.broadcasted_iota(jnp.int32, (SLOTS, SLOTS), 0)
        c = lax.broadcasted_iota(jnp.int32, (SLOTS, SLOTS), 1)
        upper = jnp.where(r <= c, 1.0, 0.0).astype(jnp.bfloat16)
        stacked = jnp.concatenate(masks, 0).astype(jnp.bfloat16)
        ranks[at : at + stacked.shape[0], :] = jnp.dot(stacked, upper, preferred_element_type=f32).astype(jnp.int32)

    spread_lane = lax.broadcasted_iota(jnp.int32, (8, SLOTS), 1)

    def find(table, base, t):
        rank = spread_lane + (SLOTS * t + 1) - base
        spot = jnp.zeros((8, SLOTS), jnp.int32)
        for bit in (64, 32, 16, 8, 4, 2, 1):
            probe = lane_gather(table, spot + (bit - 1))
            spot = jnp.where(probe < rank, spot + bit, spot)
        return jnp.where((rank >= 1) & (rank <= table[:, SLOTS - 1 : SLOTS]), spot, -1)

    every = slice(0, COLS)

    def lists_near():
        for a in range(ROWS):
            whole = [o_off[0, a] * unit, o_off[1, a] * unit, o_vel[0, a], o_vel[1, a], occ_ref[a]]
            for n in range(5):
                natural[n, a + 1, 1 : COLS + 1, :] = whole[n]
        masks = []
        for a in range(ROWS):
            low, high = extents(a)
            masks += [near(beside(a, k, every), low, high) for k in range(NEAR)]
        count_up(masks, 0)
        for a in range(ROWS):
            for g in range(COLS // 8):
                rows = slice(a * COLS + 8 * g, a * COLS + 8 * g + 8)
                base = jnp.zeros((8, 1), jnp.int32)
                for k in range(NEAR):
                    at = (a * NEAR + k) * COLS + 8 * g
                    table = ranks[at : at + 8, :]
                    for t in range(TILES):
                        code[t, k, rows, :] = find(table, base, t)
                    base = base + table[:, SLOTS - 1 : SLOTS]
                start[rows, :] = jnp.broadcast_to(base, (8, SLOTS))

    def flag(over):
        bad[0:8, :] = jnp.maximum(bad[0:8, :], jnp.broadcast_to(jnp.where(over, 1.0, 0.0), (8, SLOTS)))

    def lists_far():
        def copy_row(r, c):
            for n, f in enumerate((0, 1, 2, 3, 6)):
                natural[n, r, pl.ds(c, 1), :] = field[0][r, c, f : f + 1, :]

        def step(c, carry):
            copy_row(0, c)
            copy_row(ROWS + 1, c)
            return carry

        lax.fori_loop(0, COLS + 2, step, 0)
        for r in range(1, ROWS + 1):
            copy_row(r, 0)
            copy_row(r, COLS + 1)
        first = ROWS * NEAR * COLS
        row = lax.broadcasted_iota(jnp.int32, (COLS, 1), 0)
        masks = []
        for a in range(ROWS):
            low, high = extents(a)
            masks += [near(beside(a, k, every), low, high) for k in range(NEAR, 8)]
            masks += [jnp.where(row == b, near(beside(a, k, every), low, high), 0.0) for k, b in PAST]
        count_up(masks, first)
        width = 8 - NEAR + len(PAST)
        for a in range(ROWS):
            for g in range(COLS // 8):
                rows = slice(a * COLS + 8 * g, a * COLS + 8 * g + 8)
                base = start[rows, 0:1]
                for n in range(width):
                    past = n >= 8 - NEAR
                    k, b = PAST[n - 8 + NEAR] if past else (NEAR + n, None)
                    if past and b // 8 != g:
                        continue
                    at = first + (a * width + n) * COLS + 8 * g
                    table = ranks[at : at + 8, :]
                    for t in range(TILES):
                        found = find(table, base, t)
                        if past:
                            found = jnp.where(found >= 0, found, code[t, k, rows, :])
                        code[t, k, rows, :] = found
                    base = base + table[:, SLOTS - 1 : SLOTS]
                flag(base > TILES * SLOTS)

    field_row = lax.broadcasted_iota(jnp.int32, (FIELDS, SLOTS), 0)

    def place(v):
        if isinstance(v, int):
            if v < ROWS * INNER:
                return v // INNER, v % INNER + 1
            return (v - ROWS * INNER) // 2, (v - ROWS * INNER) % 2 * (COLS - 1)
        a = jnp.where(v >= INNER, 1, 0)
        e = v - ROWS * INNER
        last = e >= 0
        a = jnp.where(last, lax.shift_right_logical(jnp.maximum(e, 0), 1), a)
        return a, jnp.where(last, lax.bitwise_and(e, 1) * (COLS - 1), v - INNER * a + 1)

    def broadcast_own(s, c, dst):
        a, b = place(c)
        mine = own_p[2 * a + (b // 8 if isinstance(b, int) else lax.shift_right_logical(b, 3))]
        at = lax.broadcasted_iota(jnp.int32, mine.shape, 1) & 7
        mine = jnp.where(at == (b & 7), mine.astype(f32), 0.0).astype(jnp.bfloat16)
        wide = jnp.dot(mine, pick[...], preferred_element_type=f32)
        for f in range(OWN_FIELDS):
            dst[f] = wide[:, f * SLOTS : (f + 1) * SLOTS]

    def sweep(own_at, start_at, tiles, finish):
        for i0 in range(0, SLOTS, BLOCK):
            here = pl.ds(i0, BLOCK)
            own = own_at(here)
            totals = start_at(here)
            for rows in tiles:
                totals = pair_terms(own, rows, totals)
            finish(here, totals)

    def rows_of(tile):
        return [tile[f : f + 1, :] for f in range(6)]

    def from_zero(here):
        return zeros, zeros, zeros

    def own_of(bc):
        return lambda here: [bc[f, here, :] for f in range(OWN_FIELDS)]

    def to_acc(acc):
        def finish(here, totals):
            for f in range(3):
                acc[f, here, :] = totals[f]

        return finish

    along_y = [jnp.where(field_row == 1, db * unit, 0.0) for _, db in LISTED]

    def pack(s, c, t, sides_of, packed, inside):
        a, b = place(c)
        inward = 1 - 2 * a
        x_shift = jnp.where(field_row == 0, unit * (inward * 1.0), 0.0)
        for k in sides_of:
            way, db = LISTED[k]
            at_b = b + 1 + db
            if inside:
                at_b = jnp.clip(at_b, 1, COLS)
            take = jnp.broadcast_to(code[t, k, pl.ds(a * COLS + b, 1), :], (FIELDS, SLOTS))
            moved = lane_gather(field[s][a + 1 + way * inward, at_b], take & (SLOTS - 1))
            if way > 0:
                moved = moved + x_shift
            elif way < 0:
                moved = moved - x_shift
            if db:
                moved = moved + along_y[k]
            packed = jnp.where(take >= 0, moved, packed)
        return packed

    nothing = jnp.zeros((FIELDS, SLOTS), f32)

    def early(s):
        broadcast_own(s, 0, bcs[0].at[0])

        def some(u, carry):
            for n in range(WAYS):
                c = WAYS * u + n
                a, b = place(c)
                broadcast_own(s, jnp.minimum(c + 1, CELLS - 1), bcs[(n + 1) % WAYS].at[u + (n + 1) // WAYS])
                rows = [field[s][a + 1, b + 1, f : f + 1, :] for f in range(6)]
                sweep(own_of(bcs[n].at[u]), from_zero, [rows], to_acc(accs[n].at[u]))
            return carry

        lax.fori_loop(0, TURNS, some, 0)

    def collect(c, acc, valid):
        a, b = place(c)
        if valid is not True:
            b = jnp.where(valid, b, -4 * SLOTS)
        for i0 in range(0, SLOTS, BLOCK):
            here = pl.ds(i0, BLOCK)
            rates = rate_t[a, here, :]
            for f in range(3):
                rates = jnp.where(lanes == f * COLS + b, jnp.sum(acc[f, here, :], 1, keepdims=True), rates)
            rate_t[a, here, :] = rates

    def late(s, relay, rest_of_halo):
        def pack_all(c, dst):
            for t in range(TILES):
                dst[t] = pack(s, c, t, range(8), nothing, False)

        def begin(u):
            for n in range(WAYS):
                pack_all(WAYS * u + n, lates[n].at[u])

        def some(last, u, carry):
            for n in range(WAYS):
                c = WAYS * u + n
                if n == 0:
                    w = jnp.maximum(u - 1, 0)
                    collect(jnp.maximum(c - 1, 0), accs[WAYS - 1].at[w], u > 0)
                else:
                    collect(c - 1, accs[n - 1].at[u], True)
                tiles = [rows_of(lates[n].at[u, t]) for t in range(TILES)]
                acc = accs[n].at[u]

                def start_at(here):
                    return tuple(acc[f, here, :] for f in range(3))

                sweep(own_of(bcs[n].at[u]), start_at, tiles, to_acc(acc))
                pack_all(jnp.minimum(c + WAYS, last - WAYS + n), lates[n].at[u + 1])
            return carry

        begin(0)
        lax.fori_loop(0, 2, functools.partial(some, ROWS * INNER), 0)
        relay()
        lax.fori_loop(2, INNER_TURNS, functools.partial(some, ROWS * INNER), 0)
        rest_of_halo()
        begin(INNER_TURNS)
        lax.fori_loop(INNER_TURNS, TURNS, functools.partial(some, CELLS), 0)
        collect(CELLS - 1, accs[WAYS - 1].at[TURNS - 1], True)

    def update(s, step):
        for a in range(ROWS):
            rates = rate_t[a].T
            occ = occ_ref[a]
            keep = keep_ref[a]
            rho = o_den[a]
            gain = step * occ
            scale = vel_coef / (rho + 1.0 - occ)
            o_den[a] = rho + gain * (rho_coef * rho * rates[0:COLS])
            vx = (o_vel[0, a] + gain * (scale * rates[COLS : 2 * COLS])) * keep
            vy = (o_vel[1, a] + gain * (scale * rates[2 * COLS : 3 * COLS] - gravity_accel)) * keep
            o_vel[0, a] = vx
            o_vel[1, a] = vy
            o_off[0, a] = o_off[0, a] + gain * vx
            o_off[1, a] = o_off[1, a] + gain * vy

    me_a = gx * 2 + core
    me_b = plane
    for s in range(ITERS):
        fastest(s)
        copies = halo(s)
        if s == 0:
            publish(s)
            if ring:
                boxes()
                lists_near()
                turn()
            pl.semaphore_wait(barrier, len(peers_a) + len(peers_b) + len(sides))
            spread(s, peers_a, msg_a, slot_a, me_a, a_send, a_recv)
        else:
            spread(s, peers_a, msg_a, slot_a, me_a, a_send, a_recv)
            publish(s)
        for copy, (a, b) in sorted(zip(copies, SIDES), key=lambda pair: abs(pair[1][1])):
            copy.start()
        if ring:
            if s > 0:
                turn()
            early(s)

        def relay():
            gathered(s, peers_a, slot_a, a_send, a_recv).wait_recv()
            msg_b[s] = jnp.max(slot_a[s], axis=0)
            spread(s, peers_b, msg_b, slot_b, me_b, b_send, b_recv)

        if s == 0 or not ring:
            relay()
        for copy, (a, b) in zip(copies, SIDES):
            if b == 0:
                copy.wait_recv()
        clear_rows(s)

        def rest_of_halo():
            for copy, (a, b) in zip(copies, SIDES):
                if b != 0:
                    copy.wait_recv()
            clear_columns(s)

        if not ring:
            rest_of_halo()
            dense(s)
        elif s == 0:
            rest_of_halo()
            lists_far()
            late(s, lambda: None, lambda: None)
        else:
            late(s, relay, rest_of_halo)
        gathered(s, peers_b, slot_b, b_send, b_recv).wait_recv()
        result = jnp.max(slot_b[s], axis=0)
        top = 10.0 + jnp.sqrt(result[:, 0:1])
        update(s, courant * smoothing / top)
        if ring and s < ITERS - 1:
            check()
        for copy in copies:
            copy.wait_send()
        gathered(s, peers_a, slot_a, a_send, a_recv).wait_send()
        gathered(s, peers_b, slot_b, b_send, b_recv).wait_send()
    o_flag[0, 0] = jnp.max(result[:, SLOTS // 2 :])


def substeps(ring, n_gx, n_gy, offsets, density, velocity, counts, walls):
    shape = jax.ShapeDtypeStruct
    dma = pltpu.SemaphoreType.DMA
    f32 = jnp.float32
    n_a, n_b = 2 * n_gx, n_gy // 2
    if ring:
        extra = [
            pltpu.VMEM((2 * ROWS, SLOTS, SLOTS), jnp.bfloat16),
            pltpu.VMEM((SLOTS, OWN_FIELDS * SLOTS), jnp.bfloat16),
            pltpu.VMEM((TILES, 8, CELLS, SLOTS), jnp.int32),
            pltpu.VMEM((5, ROWS + 2, 24, SLOTS), f32),
            pltpu.VMEM((ROWS * (8 + len(PAST)) * COLS, SLOTS), jnp.int32),
            pltpu.VMEM((CELLS, SLOTS), jnp.int32),
            pltpu.VMEM((2, ROWS, COLS, SLOTS), f32),
            pltpu.VMEM((2, ROWS, COLS, SLOTS), f32),
            pltpu.VMEM((COLS, SLOTS), f32),
        ]
        for per_cell in ((OWN_FIELDS, SLOTS, SLOTS), (3, SLOTS, SLOTS), (TILES, FIELDS, SLOTS)):
            extra += [pltpu.VMEM((TURNS + 1,) + per_cell, f32)] * WAYS
    else:
        extra = [pltpu.VMEM((ROWS, SLOTS, SLOTS), f32)]
    return pl.pallas_call(
        functools.partial(kernel, ring),
        out_shape=(
            shape(offsets.shape, f32),
            shape(density.shape, f32),
            shape(velocity.shape, f32),
            shape((1, 1), f32),
        ),
        in_specs=[pl.BlockSpec(memory_space=pltpu.VMEM)] * 5,
        out_specs=tuple(pl.BlockSpec(memory_space=pltpu.VMEM) for _ in range(3)) + (pl.BlockSpec(memory_space=pltpu.SMEM),),
        scratch_shapes=[
            pltpu.VMEM((ROWS + 2, COLS + 2, FIELDS, SLOTS), f32),
            pltpu.VMEM((ROWS + 2, COLS + 2, FIELDS, SLOTS), f32),
            pltpu.VMEM((ROWS + 2, COLS + 2, FIELDS, SLOTS), f32),
            pltpu.VMEM((ROWS, SLOTS, SLOTS), f32),
            pltpu.VMEM((ROWS, COLS, SLOTS), f32),
            pltpu.VMEM((ROWS, COLS, SLOTS), f32),
            pltpu.VMEM((ITERS, 1, SLOTS), f32),
            pltpu.VMEM((ITERS, 1, SLOTS), f32),
            pltpu.VMEM((ITERS, n_a, 1, SLOTS), f32),
            pltpu.VMEM((ITERS, n_b, 1, SLOTS), f32),
            dma((ITERS, 8)),
            dma((ITERS, 8)),
            dma((ITERS,)),
            dma((ITERS,)),
            dma((ITERS,)),
            dma((ITERS,)),
        ]
        + extra,
        compiler_params=pltpu.CompilerParams(collective_id=0 if ring else 1, has_side_effects=True),
    )(offsets, density, velocity, counts, walls)


def shards(n_gx, n_gy, *args):
    *fast, flag = substeps(True, n_gx, n_gy, *args)
    return lax.cond(
        flag[0, 0] > 0.0,
        lambda: tuple(substeps(False, n_gx, n_gy, *args)[:3]),
        lambda: tuple(fast),
    )


def solution(mesh):
    fields = P(None, "gx", "gy", None)
    cells = P("gx", "gy")
    return jax.shard_map(
        functools.partial(shards, mesh.shape["gx"], mesh.shape["gy"]),
        mesh=mesh,
        in_specs=(fields, P("gx", "gy", None), fields, cells, cells),
        out_specs=(fields, P("gx", "gy", None), fields),
        check_vma=False,
    )
```
